512 devices in a mesh: space: 64 (over z, x), member: 8 (over y, core).
Axes of the slice: x: 4, y: 4, z: 16, core: 2. Of those that a mesh axis runs over, the one named last changes fastest.
Arguments:
- spectra: float32 [16, 36, 256, 720], P('member', None, 'space'), may hold values from 0.5 to 2
- group_speed: float32 [256, 720], P('space'), may hold values from 0.15 to 0.5
- turning_rate: float32 [256, 720], P('space'), may hold values from -0.28 to 0.28
- obs_cell: int32 [2, 1024], replicated, may hold values from 0 to 184319, as said below
- obs_value: float32 [2, 1024], replicated, may hold values from 0.9 to 1.6
- obs_variance: float32 [2, 1024], replicated, may hold values from 0.001 to 0.01
Outputs:
- analysis: float32 [16, 36, 184320], P(None, None, ('space', 'member'))
The draws below stay inside these ranges and needn't reach their ends.
Inputs may be any that keep to these rules, and one draw needn't show every extreme that they name: `obs_cell`: every block of 360 consecutive cells starting at a multiple of 360 holds the cell of at least one observation in every batch.
All inputs are finite; a program needn't handle non-finite values.
Results may differ from the reference program's by a relative error of at most 0.0003.
Values sent between devices are 32-bit elements; how exact they have to be, the bound alone decides.
A program may use at most 64 MiB of HBM per device.

```python
import math
import jax
import jax.numpy as jnp
from jax import lax

DIRS = 36
LON = 720
STEPS = 4
NOBS = 1024
BATCHES = 2
MEMBERS = 16
LAT = 256
CELLS = 184320
OWN = 360
LOC = 4


def draw_obs_cell(key, part):
    devices = CELLS // OWN
    batches_drawn = []
    for batch in range(BATCHES):
        folded = jax.random.fold_in(key, 7 + batch)
        first_key, second_key, third_key = jax.random.split(folded, 3)
        placed = jnp.arange(devices, dtype=jnp.int32) * OWN + jax.random.randint(first_key, (devices,), 0, OWN, dtype=jnp.int32)
        others = jax.random.randint(second_key, (NOBS - devices,), 0, CELLS, dtype=jnp.int32)
        joined = jnp.concatenate([placed, others])
        batches_drawn.append(jax.random.permutation(third_key, joined))
    return jnp.stack(batches_drawn)


def level_of(rng, shape, cuts, least, largest):
    level = 1.0
    for axis_at, parts in cuts:
        steps = jax.random.uniform(jax.random.fold_in(jax.random.fold_in(rng, 6), axis_at), (parts,), jnp.float32, least / len(cuts), largest / len(cuts))
        level = level * jnp.repeat(jnp.exp(steps), shape[axis_at] // parts).reshape((-1,) + (1,) * (len(shape) - 1 - axis_at))
    return level


def setup_inputs(seed: int = 0) -> dict:
    arg_keys = jax.random.split(jax.random.key(seed), 7)
    spectra = jnp.clip(0.5 + 1.5 * jax.random.uniform(arg_keys[0], (MEMBERS, DIRS, LAT, LON), jnp.float32) ** level_of(arg_keys[0], (MEMBERS, DIRS, LAT, LON), ((0, 8), (2, 64)), -0.2, 0.2), 0.5, 2.0)
    group_speed = jnp.clip(0.15 + 0.35 * jax.random.uniform(arg_keys[1], (LAT, LON), jnp.float32) ** level_of(arg_keys[1], (LAT, LON), ((0, 64),), -0.2, 0.2), 0.15, 0.5)
    turning_rate = jnp.clip(jax.random.uniform(arg_keys[2], (LAT, LON), jnp.float32, -0.28, 0.28) * level_of(arg_keys[2], (LAT, LON), ((0, 64),), -0.4, 0.0), -0.28, 0.28)
    obs_cell = draw_obs_cell(jax.random.fold_in(arg_keys[6], 71), 0)
    obs_value = jnp.clip(jax.random.uniform(arg_keys[4], (BATCHES, NOBS), jnp.float32, 0.9, 1.6), 0.9, 1.6)
    obs_variance = jnp.clip(jnp.exp(jax.random.uniform(arg_keys[5], (BATCHES, NOBS), jnp.float32, math.log(0.001), math.log(0.01))), 0.001, 0.01)
    return dict(spectra=spectra, group_speed=group_speed, turning_rate=turning_rate, obs_cell=obs_cell, obs_value=obs_value, obs_variance=obs_variance)


HIGH = lax.Precision.HIGHEST

def transport(padded, speed, turning, cosines, sines):
    centre = padded[:, :, 1:-1, :]
    south = padded[:, :, :-2, :]
    north = padded[:, :, 2:, :]
    along_x = speed[None] * cosines[:, None, None]
    along_y = speed[None] * sines[:, None, None]
    along_turn = turning[None] * cosines[:, None, None]
    west = jnp.roll(centre, 1, axis=3)
    east = jnp.roll(centre, -1, axis=3)
    behind = jnp.roll(centre, 1, axis=1)
    ahead = jnp.roll(centre, -1, axis=1)
    result = centre - jnp.maximum(along_x, 0.0) * (centre - west) - jnp.minimum(along_x, 0.0) * (east - centre)
    result = result - jnp.maximum(along_y, 0.0) * (centre - south) - jnp.minimum(along_y, 0.0) * (north - centre)
    result = result - jnp.maximum(along_turn, 0.0) * (centre - behind) - jnp.minimum(along_turn, 0.0) * (ahead - centre)
    return result

def panel(prior, values, variance):
    members = prior.shape[1]
    centre = lax.optimization_barrier(jnp.mean(prior, axis=1))
    anomaly = prior - centre[:, None]
    spread = lax.optimization_barrier(jnp.sum(anomaly * anomaly, axis=1)) / (members - 1)
    total = spread + variance
    shrink = 1.0 / (1.0 + jnp.sqrt(variance / total))
    weights_obs = ((values - centre)[:, None] - shrink[:, None] * anomaly) / total[:, None]
    outer = anomaly[:, :, None] * weights_obs[:, None, :]
    return outer.reshape(prior.shape[0], members * members) / (members - 1)

def taper(cell_ids, targets):
    lat_gap = cell_ids[:, None] // LON - targets[None, :] // LON
    lon_gap = jnp.abs(cell_ids[:, None] % LON - targets[None, :] % LON)
    lon_gap = jnp.minimum(lon_gap, LON - lon_gap)
    square = (lat_gap * lat_gap + lon_gap * lon_gap).astype(jnp.float32)
    near = jnp.maximum(1.0 - square / (LOC * LOC), 0.0)
    return near * near

def reference(spectra, group_speed, turning_rate, obs_cell, obs_value, obs_variance):
    members = spectra.shape[0]
    angles = 2.0 * math.pi * jnp.arange(DIRS, dtype=jnp.float32) / DIRS
    cosines = jnp.cos(angles)
    sines = jnp.sin(angles)
    energy = spectra
    for step in range(STEPS):
        padded = jnp.pad(energy, ((0, 0), (0, 0), (1, 1), (0, 0)))
        energy = transport(padded, group_speed, turning_rate, cosines, sines)
    state = energy.reshape(members, DIRS, CELLS)
    blocks = CELLS // OWN
    for batch in range(BATCHES):
        targets = obs_cell[batch]
        mean_dir = lax.optimization_barrier(jnp.mean(state, axis=1))
        prior = jnp.take(mean_dir, targets, axis=1).T
        mixing = panel(prior, obs_value[batch], obs_variance[batch])
        deviation = state - lax.optimization_barrier(jnp.mean(state, axis=0, keepdims=True))

        def one_block(index):
            start = (index * OWN).astype(jnp.int32)
            cell_ids = start + jnp.arange(OWN, dtype=jnp.int32)
            gain = jnp.dot(taper(cell_ids, targets), mixing, precision=HIGH).reshape(OWN, members, members)
            piece = lax.dynamic_slice_in_dim(deviation, start, OWN, 2)
            return jnp.einsum('kdc,ckl->ldc', piece, gain, precision=HIGH)
        updates = lax.map(one_block, jnp.arange(blocks, dtype=jnp.int32))
        state = state + jnp.transpose(updates, (1, 2, 0, 3)).reshape(members, DIRS, CELLS)
    return state
```

```python
import functools
import math

import jax
import jax.numpy as jnp
from jax import lax
from jax.experimental import pallas as pl
from jax.experimental.pallas import tpu as pltpu
from jax.sharding import PartitionSpec as P

LON = 720
STEPS = 4
BATCHES = 2
LOC = 4
DIRS = 36
NOBS = 1024
MEMBERS = 16
ROWS = 4
OWN = 360
WIDE = 768
TALL = 48
BASE = 8
PART = 384
HALF = 24
CHUNK = 512
F32 = jnp.float32
BF16 = jnp.bfloat16


def step_row(centre, behind, ahead, upwind_y, cx, cy, cr, pick_x):
    west = pltpu.roll(centre, 1, axis=1)
    east = pltpu.roll(centre, WIDE - 1, axis=1)
    result = centre - cx * (centre - jnp.where(pick_x, west, east))
    result = result - cy * (centre - upwind_y)
    return result - jnp.abs(cr) * (centre - jnp.where(cr > 0.0, behind, ahead))


def wave_kernel(
    spaces, peers,
    x_ref, speed_ref, turn_ref, trig_ref, obs_ref,
    state_ref, prior_ref,
    e_ref, south_ref, north_ref, cx_ref, cy_ref, cr_ref, send_ref, mean_ref,
    mine_ref, near_ref, sum_ref,
    halo_send, halo_recv, part_send, part_recv, near_send, near_recv,
    all_send, all_recv, own_sem,
):
    space = lax.axis_index("space")
    member = lax.axis_index("member")
    shifts = (1, spaces - 1, 2, spaces - 2)

    barrier = pltpu.get_barrier_semaphore()
    for shift in shifts:
        pl.semaphore_signal(
            barrier, inc=1, device_id=(lax.rem(space + shift, spaces), member),
            device_id_type=pl.DeviceIdType.MESH)
    for offset in range(1, peers):
        pl.semaphore_signal(
            barrier, inc=1, device_id=(space, lax.rem(member + offset, peers)),
            device_id_type=pl.DeviceIdType.MESH)
    pl.semaphore_wait(barrier, len(shifts) + peers - 1)

    def held(step, m, r):
        return x_ref.at[m, r] if step == 0 else e_ref.at[step - 1, m, r]

    def halo(step, m, side):
        if side == 0:
            source = held(step, m, ROWS - 1).at[pl.ds(BASE, HALF)]
            target, to = south_ref.at[step, m], lax.rem(space + 1, spaces)
        else:
            source = held(step, m, 0).at[pl.ds(BASE + 16, HALF)]
            target, to = north_ref.at[step, m], lax.rem(space + spaces - 1, spaces)
        return pltpu.make_async_remote_copy(
            src_ref=source, dst_ref=target,
            send_sem=halo_send.at[step, m, side], recv_sem=halo_recv.at[step, m, side],
            device_id=(to, member), device_id_type=pl.DeviceIdType.MESH)

    for m in range(2):
        for side in range(2):
            halo(0, m, side).start()

    cosines = jnp.concatenate([trig_ref[0]] * (WIDE // 128), axis=1)
    sines = jnp.concatenate([trig_ref[1]] * (WIDE // 128), axis=1)
    for r in range(ROWS):
        speed = speed_ref[r:r + 1, :]
        cx_ref[r] = speed * jnp.abs(cosines)
        cy_ref[r] = speed * jnp.abs(sines)
        cr_ref[r] = turn_ref[r:r + 1, :] * cosines
    pick_x = cosines > 0.0
    pick_y = sines > 0.0
    has_south = (space > 0).astype(F32)
    has_north = (space < spaces - 1).astype(F32)

    def advance(step, m, r):
        centre = held(step, m, r)[BASE:BASE + DIRS, :]
        behind = held(step, m, r)[BASE - 1:BASE - 1 + DIRS, :]
        ahead = held(step, m, r)[BASE + 1:BASE + 1 + DIRS, :]
        if r > 0:
            south = held(step, m, r - 1)[BASE:BASE + DIRS, :]
        if r < ROWS - 1:
            north = held(step, m, r + 1)[BASE:BASE + DIRS, :]
        if r == 0:
            south = jnp.concatenate([south_ref[step, m] * has_south, north[HALF:]], axis=0)
        if r == ROWS - 1:
            north = jnp.concatenate(
                [south[:16], (north_ref[step, m] * has_north)[:DIRS - 16]], axis=0)
        new = step_row(centre, behind, ahead, jnp.where(pick_y, south, north),
                       cx_ref[r], cy_ref[r], cr_ref[r], pick_x)
        e_ref[step, m, r, BASE:BASE + DIRS, :] = new
        e_ref[step, m, r, BASE - 1:BASE, :] = new[DIRS - 1:DIRS]
        e_ref[step, m, r, BASE + DIRS:BASE + DIRS + 1, :] = new[0:1]
        if step == STEPS - 1:
            mean_ref[m * ROWS + r:m * ROWS + r + 1, :] = (
                jnp.sum(new, axis=0, keepdims=True) * (1.0 / DIRS))
            send_ref[2 * r, m * DIRS:(m + 1) * DIRS, :] = new[:, :PART]
            send_ref[2 * r + 1, m * DIRS:(m + 1) * DIRS, :] = pltpu.roll(
                new, WIDE - OWN, axis=1)[:, :PART]

    cuts = ((0, 32), (32, 40))

    def part(m, offset):
        to = lax.rem(member + offset, peers)
        first, rows = cuts[m]
        return pltpu.make_async_remote_copy(
            src_ref=send_ref.at[to, pl.ds(first, rows)],
            dst_ref=state_ref.at[member, pl.ds(first, rows)],
            send_sem=part_send.at[m, offset], recv_sem=part_recv.at[m, offset],
            device_id=(space, to), device_id_type=pl.DeviceIdType.MESH)

    order = (4, 3, 5, 2, 6, 1, 7)
    for step in range(STEPS):
        for m in range(2):
            for r in range(1, ROWS - 1):
                advance(step, m, r)
            halo(step, m, 0).wait_recv()
            advance(step, m, 0)
            if step < STEPS - 1:
                halo(step + 1, m, 1).start()
            halo(step, m, 1).wait_recv()
            advance(step, m, ROWS - 1)
            if step < STEPS - 1:
                halo(step + 1, m, 0).start()
            else:
                for offset in order:
                    part(m, offset).start()
    own = pltpu.make_async_copy(send_ref.at[member], state_ref.at[member], own_sem)
    own.start()

    mean = mean_ref[...]
    high = mean.astype(BF16)
    rest = mean - high.astype(F32)
    middle = rest.astype(BF16)
    low = (rest - middle.astype(F32)).astype(BF16)
    where_lon = lax.broadcasted_iota(jnp.int32, (WIDE, CHUNK), 0).astype(F32)
    slab = (space * ROWS).astype(F32)
    for chunk in range(BATCHES * NOBS // CHUNK):
        batch, part_of = divmod(chunk, NOBS // CHUNK)
        lanes = slice(part_of * CHUNK, (part_of + 1) * CHUNK)
        onehot = jnp.where(where_lon == obs_ref[2 * batch + 1:2 * batch + 2, lanes], 1.0, 0.0)
        onehot = onehot.astype(BF16)
        found = (
            jnp.dot(high, onehot, preferred_element_type=F32)
            + jnp.dot(middle, onehot, preferred_element_type=F32)
            + jnp.dot(low, onehot, preferred_element_type=F32))
        row = obs_ref[2 * batch:2 * batch + 1, lanes] - slab
        for m in range(2):
            value = jnp.zeros((1, CHUNK), F32)
            for r in range(ROWS):
                value = value + jnp.where(row == float(r), found[m * ROWS + r:m * ROWS + r + 1], 0.0)
            mine_ref[m * 4 + chunk:m * 4 + chunk + 1, :] = value

    def near(index):
        return pltpu.make_async_remote_copy(
            src_ref=mine_ref, dst_ref=near_ref.at[index],
            send_sem=near_send.at[index], recv_sem=near_recv.at[index],
            device_id=(lax.rem(space + shifts[index], spaces), member),
            device_id_type=pl.DeviceIdType.MESH)

    for index in range(4):
        near(index).start()
    for index in range(4):
        near(index).wait_recv()
    sum_ref[...] = mine_ref[...] + near_ref[0] + near_ref[1] + near_ref[2] + near_ref[3]
    prior_ref[member] = sum_ref[...]

    def everyone(offset):
        return pltpu.make_async_remote_copy(
            src_ref=sum_ref, dst_ref=prior_ref.at[member],
            send_sem=all_send.at[offset], recv_sem=all_recv.at[offset],
            device_id=(space, lax.rem(member + offset, peers)),
            device_id_type=pl.DeviceIdType.MESH)

    for offset in order:
        everyone(offset).start()
    for step in range(STEPS):
        for m in range(2):
            for side in range(2):
                halo(step, m, side).wait_send()
    own.wait()
    for index in range(4):
        near(index).wait_send()
    for m in range(2):
        for offset in order:
            part(m, offset).wait()
    for offset in order:
        everyone(offset).wait()


def propagate(x, speed, turn, trig, obs, spaces, peers):
    vmem = pl.BlockSpec(memory_space=pltpu.VMEM)
    dma = pltpu.SemaphoreType.DMA
    return pl.pallas_call(
        functools.partial(wave_kernel, spaces, peers),
        out_shape=(
            jax.ShapeDtypeStruct((peers, 2 * DIRS, PART), F32),
            jax.ShapeDtypeStruct((peers, 8, CHUNK), F32),
        ),
        in_specs=[vmem] * 5,
        out_specs=(vmem, vmem),
        scratch_shapes=[
            pltpu.VMEM((STEPS, 2, ROWS, TALL, WIDE), F32),
            pltpu.VMEM((STEPS, 2, HALF, WIDE), F32),
            pltpu.VMEM((STEPS, 2, HALF, WIDE), F32),
            pltpu.VMEM((ROWS, DIRS, WIDE), F32),
            pltpu.VMEM((ROWS, DIRS, WIDE), F32),
            pltpu.VMEM((ROWS, DIRS, WIDE), F32),
            pltpu.VMEM((2 * ROWS, 2 * DIRS, PART), F32),
            pltpu.VMEM((2 * ROWS, WIDE), F32),
            pltpu.VMEM((8, CHUNK), F32),
            pltpu.VMEM((4, 8, CHUNK), F32),
            pltpu.VMEM((8, CHUNK), F32),
            dma((STEPS, 2, 2)), dma((STEPS, 2, 2)),
            dma((2, 8)), dma((2, 8)),
            dma((4,)), dma((4,)),
            dma((8,)), dma((8,)),
            dma(()),
        ],
        compiler_params=pltpu.CompilerParams(collective_id=0, has_side_effects=True),
        name="propagate",
    )(x, speed, turn, trig, obs)


def panel(prior, values, variance):
    centre = jnp.sum(prior, axis=0, keepdims=True) * (1.0 / MEMBERS)
    anomaly = prior - centre
    spread = jnp.sum(anomaly * anomaly, axis=0, keepdims=True) * (1.0 / (MEMBERS - 1))
    total = spread + variance
    shrink = 1.0 / (1.0 + jnp.sqrt(variance / total))
    coef = ((values - centre) - shrink * anomaly) / (total * (MEMBERS - 1))
    return anomaly, coef


def split_mix(anomaly, coef, high_ref, low_ref):
    for l in range(MEMBERS):
        mix = anomaly * coef[l:l + 1]
        high = mix.astype(BF16)
        high_ref[l * MEMBERS:(l + 1) * MEMBERS, :] = high
        low_ref[l * MEMBERS:(l + 1) * MEMBERS, :] = (mix - high.astype(F32)).astype(BF16)


def taper(row, lon, rows, lons):
    lat_gap = row - rows
    lon_gap = jnp.abs(lon - lons)
    lon_gap = jnp.minimum(lon_gap, LON - lon_gap)
    near = jnp.maximum(1.0 - (lat_gap * lat_gap + lon_gap * lon_gap) * (1.0 / (LOC * LOC)), 0.0)
    return (near * near).astype(BF16)


def mixed(high_ref, low_ref, weights):
    dims = (((1,), (1,)), ((), ()))
    return lax.dot_general(
        high_ref[...], weights, dims, preferred_element_type=F32
    ) + lax.dot_general(low_ref[...], weights, dims, preferred_element_type=F32)


def analyse_kernel(
    peers, state_ref, block_ref, obs_ref, out_ref,
    s_ref, d_ref, prior_ref, next_ref, high_ref, low_ref, gain_ref, column_ref,
):
    device = lax.axis_index("space") * peers + lax.axis_index("member")
    own_row = (device // 2).astype(F32)
    own_lon = ((device % 2) * OWN).astype(F32)
    for k in range(MEMBERS):
        first = (k % 2) * DIRS
        s_ref[k] = state_ref[k // 2, first:first + DIRS, :]
        for chunk in range(4):
            at = (k % 2) * 4 + chunk
            prior_ref[k:k + 1, chunk * CHUNK:(chunk + 1) * CHUNK] = block_ref[k // 2, at:at + 1, :]
    column_ref[...] = jnp.transpose(obs_ref[...])

    cell_lon = lax.broadcasted_iota(jnp.int32, (PART, 128), 0).astype(F32) + own_lon
    cell_lon = jnp.concatenate([cell_lon] * (NOBS // 128), axis=1)

    def assimilate(batch, last):
        weights = taper(own_row, cell_lon, obs_ref[2 * batch:2 * batch + 1, :],
                        obs_ref[2 * batch + 1:2 * batch + 2, :])
        gain_ref[...] = mixed(high_ref, low_ref, weights).reshape(MEMBERS, MEMBERS, PART)
        mean = s_ref[0]
        for k in range(1, MEMBERS):
            mean = mean + s_ref[k]
        mean = mean * (1.0 / MEMBERS)
        for k in range(MEMBERS):
            d_ref[k] = s_ref[k] - mean

        def one(l, carry):
            for tile in range(PART // 128):
                lanes = slice(tile * 128, (tile + 1) * 128)
                total = s_ref[l, :, lanes]
                gain = gain_ref[l, :, lanes]
                for k in range(MEMBERS):
                    total = total + d_ref[k, :, lanes] * gain[k:k + 1]
                if last:
                    count = min(128, OWN - tile * 128)
                    out_ref[l, :, tile * 128:tile * 128 + count] = total[:, :count]
                else:
                    s_ref[l, :, lanes] = total
            return carry

        lax.fori_loop(0, MEMBERS, one, 0)

    anomaly, coef = panel(prior_ref[:, :NOBS], obs_ref[4:5, :], obs_ref[6:7, :])
    split_mix(anomaly, coef, high_ref, low_ref)
    width = 256
    for at in range(0, NOBS, width):
        weights = taper(column_ref[at:at + width, 2:3], column_ref[at:at + width, 3:4],
                        obs_ref[0:1, :], obs_ref[1:2, :])
        gain = mixed(high_ref, low_ref, weights)
        prior = prior_ref[:, NOBS + at:NOBS + at + width]
        deviation = prior - jnp.sum(prior, axis=0, keepdims=True) * (1.0 / MEMBERS)
        for l in range(MEMBERS):
            next_ref[l:l + 1, at:at + width] = prior[l:l + 1] + jnp.sum(
                deviation * gain[l * MEMBERS:(l + 1) * MEMBERS], axis=0, keepdims=True)
    assimilate(0, False)
    anomaly, coef = panel(next_ref[...], obs_ref[5:6, :], obs_ref[7:8, :])
    split_mix(anomaly, coef, high_ref, low_ref)
    assimilate(1, True)


def analyse(state, blocks, obs, peers):
    vmem = pl.BlockSpec(memory_space=pltpu.VMEM)
    return pl.pallas_call(
        functools.partial(analyse_kernel, peers),
        out_shape=jax.ShapeDtypeStruct((MEMBERS, DIRS, OWN), F32),
        in_specs=[vmem] * 3,
        out_specs=vmem,
        scratch_shapes=[
            pltpu.VMEM((MEMBERS, DIRS, PART), F32),
            pltpu.VMEM((MEMBERS, DIRS, PART), F32),
            pltpu.VMEM((MEMBERS, BATCHES * NOBS), F32),
            pltpu.VMEM((MEMBERS, NOBS), F32),
            pltpu.VMEM((MEMBERS * MEMBERS, NOBS), BF16),
            pltpu.VMEM((MEMBERS * MEMBERS, NOBS), BF16),
            pltpu.VMEM((MEMBERS, MEMBERS, PART), F32),
            pltpu.VMEM((NOBS, 8), F32),
        ],
        name="analyse",
    )(state, blocks, obs)


def widen(array):
    return jnp.concatenate([array, array[..., :24], array[..., -24:]], axis=-1)


def per_device(spectra, group_speed, turning_rate, obs_cell, obs_value, obs_variance):
    spaces, peers = lax.axis_size("space"), lax.axis_size("member")
    angles = 2.0 * math.pi * jnp.arange(DIRS, dtype=F32) / DIRS
    trig = jnp.broadcast_to(jnp.stack([jnp.cos(angles), jnp.sin(angles)])[:, :, None], (2, DIRS, 128))
    x = jnp.transpose(spectra, (0, 2, 1, 3))
    x = widen(jnp.concatenate([x[:, :, -BASE:], x, x[:, :, :TALL - BASE - DIRS]], axis=2))
    rows = (obs_cell // LON).astype(F32)
    lons = (obs_cell % LON).astype(F32)
    places = jnp.stack([rows, lons], axis=1).reshape(2 * BATCHES, NOBS)
    obs = jnp.concatenate([places, obs_value, obs_variance], axis=0)
    state, blocks = propagate(x, widen(group_speed), widen(turning_rate), trig, obs, spaces, peers)
    return analyse(state, blocks, obs, peers)


def solution(mesh):
    placed = (P("member", None, "space", None), P("space", None), P("space", None), P(), P(), P())
    return jax.shard_map(
        per_device,
        mesh=mesh,
        in_specs=placed,
        out_specs=P(None, None, ("space", "member")),
        check_vma=False,
    )
```

```python
import functools
import math

import jax
import jax.numpy as jnp
import numpy as np
from jax import lax
from jax.experimental import pallas as pl
from jax.experimental.pallas import tpu as pltpu
from jax.sharding import PartitionSpec as P

LON = 720
STEPS = 4
BATCHES = 2
LOC = 4
DIRS = 36
NOBS = 1024
MEMBERS = 16
ROWS = 4
OWN = 360
WIDE = 768
TALL = 48
BASE = 8
PART = 384
HALF = 24
CHUNK = 512
F32 = jnp.float32
BF16 = jnp.bfloat16


def step_row(centre, behind, ahead, upwind_y, cx, cy, cr, pick_x):
    west = pltpu.roll(centre, 1, axis=1)
    east = pltpu.roll(centre, WIDE - 1, axis=1)
    result = centre - cx * (centre - jnp.where(pick_x, west, east))
    result = result - cy * (centre - upwind_y)
    return result - jnp.abs(cr) * (centre - jnp.where(cr > 0.0, behind, ahead))


def widen(array):
    return jnp.concatenate([array, array[:, :24], array[:, LON - 24:]], axis=1)


def panel(prior, values, variance):
    centre = jnp.sum(prior, axis=0, keepdims=True) * (1.0 / MEMBERS)
    anomaly = prior - centre
    spread = jnp.sum(anomaly * anomaly, axis=0, keepdims=True) * (1.0 / (MEMBERS - 1))
    total = spread + variance
    shrink = 1.0 / (1.0 + jnp.sqrt(variance / total))
    coef = ((values - centre) - shrink * anomaly) / (total * (MEMBERS - 1))
    return anomaly, coef


def split_mix(anomaly, coef, high_ref, low_ref):
    for l in range(MEMBERS):
        mix = anomaly * coef[l:l + 1]
        high = mix.astype(BF16)
        high_ref[l * MEMBERS:(l + 1) * MEMBERS, :] = high
        low_ref[l * MEMBERS:(l + 1) * MEMBERS, :] = (mix - high.astype(F32)).astype(BF16)


def taper(row, lon, rows, lons):
    lat_gap = row - rows
    lon_gap = jnp.abs(lon - lons)
    lon_gap = jnp.minimum(lon_gap, LON - lon_gap)
    near = jnp.maximum(1.0 - (lat_gap * lat_gap + lon_gap * lon_gap) * (1.0 / (LOC * LOC)), 0.0)
    return (near * near).astype(BF16)


def mixed(high_ref, low_ref, weights):
    dims = (((1,), (1,)), ((), ()))
    return lax.dot_general(
        high_ref[...], weights, dims, preferred_element_type=F32
    ) + lax.dot_general(low_ref[...], weights, dims, preferred_element_type=F32)


def wave_kernel(
    spaces, peers,
    x_ref, speed_ref, turn_ref, trig_ref, cell_ref, value_ref, variance_ref,
    out_ref,
    e_ref, south_ref, north_ref, cx_ref, cy_ref, cr_ref, send_ref, mean_ref,
    mine_ref, near_ref, sum_ref, state_ref, block_ref, place_ref, column_ref,
    cross_ref, taper_ref, onehot_ref, s_ref, prior_ref, next_ref,
    high_ref, low_ref, gain_ref, total_ref,
    halo_send, halo_recv, part_send, part_recv, near_send, near_recv,
    all_send, all_recv, own_sem,
):
    space = lax.axis_index("space")
    member = lax.axis_index("member")
    shifts = (1, spaces - 1, 2, spaces - 2)

    barrier = pltpu.get_barrier_semaphore()
    for shift in shifts:
        pl.semaphore_signal(
            barrier, inc=1, device_id=(lax.rem(space + shift, spaces), member),
            device_id_type=pl.DeviceIdType.MESH)
    for offset in range(1, peers):
        pl.semaphore_signal(
            barrier, inc=1, device_id=(space, lax.rem(member + offset, peers)),
            device_id_type=pl.DeviceIdType.MESH)

    def keep(step, m, r, new):
        e_ref[step, m, r, BASE:BASE + DIRS, :] = new
        e_ref[step, m, r, BASE - 1:BASE, :] = new[DIRS - 1:DIRS]
        e_ref[step, m, r, BASE + DIRS:BASE + DIRS + 1, :] = new[0:1]

    for r in (0, ROWS - 1, 1, 2):
        for m in range(2):
            keep(0, m, r, widen(x_ref[m, r]))
    pl.semaphore_wait(barrier, len(shifts) + peers - 1)

    def halo(step, m, side):
        if side == 0:
            source = e_ref.at[step, m, ROWS - 1, pl.ds(BASE, HALF)]
            target, to = south_ref.at[step, m], lax.rem(space + 1, spaces)
        else:
            source = e_ref.at[step, m, 0, pl.ds(BASE + 16, HALF)]
            target, to = north_ref.at[step, m], lax.rem(space + spaces - 1, spaces)
        return pltpu.make_async_remote_copy(
            src_ref=source, dst_ref=target,
            send_sem=halo_send.at[step, m, side], recv_sem=halo_recv.at[step, m, side],
            device_id=(to, member), device_id_type=pl.DeviceIdType.MESH)

    for m in range(2):
        for side in range(2):
            halo(0, m, side).start()

    cosines = jnp.concatenate([trig_ref[0]] * (WIDE // 128), axis=1)
    sines = jnp.concatenate([trig_ref[1]] * (WIDE // 128), axis=1)
    speeds = widen(speed_ref[...])
    turns = widen(turn_ref[...])
    for r in range(ROWS):
        cx_ref[r] = speeds[r:r + 1, :] * jnp.abs(cosines)
        cy_ref[r] = speeds[r:r + 1, :] * jnp.abs(sines)
        cr_ref[r] = turns[r:r + 1, :] * cosines
    pick_x = cosines > 0.0
    pick_y = sines > 0.0
    has_south = (space > 0).astype(F32)
    has_north = (space < spaces - 1).astype(F32)

    cells = cell_ref[...].astype(F32)
    rows = jnp.floor((cells + 0.5) * (1.0 / LON))
    lons = cells - rows * float(LON)
    place_ref[...] = jnp.concatenate([rows, lons, rows, lons], axis=0)
    column_ref[...] = jnp.transpose(place_ref[...])

    device = space * peers + member
    own_row = (device // 2).astype(F32)
    own_lon = ((device % 2) * OWN).astype(F32)

    def own_taper(batch):
        cell_lon = lax.broadcasted_iota(jnp.int32, (PART, 128), 0).astype(F32) + own_lon
        cell_lon = jnp.concatenate([cell_lon] * (NOBS // 128), axis=1)
        taper_ref[batch] = taper(own_row, cell_lon, place_ref[batch:batch + 1, :],
                                 place_ref[2 + batch:3 + batch, :])

    width = 256

    def cross_taper(at):
        cross_ref[at:at + width, :] = taper(
            column_ref[at:at + width, 1:2], column_ref[at:at + width, 3:4],
            place_ref[0:1, :], place_ref[2:3, :])

    def select(chunk):
        batch, part_of = divmod(chunk, NOBS // CHUNK)
        lanes = slice(part_of * CHUNK, (part_of + 1) * CHUNK)
        where_lon = lax.broadcasted_iota(jnp.int32, (WIDE, CHUNK), 0).astype(F32)
        onehot_ref[chunk] = jnp.where(
            where_lon == place_ref[2 + batch:3 + batch, lanes], 1.0, 0.0).astype(BF16)

    filler = {
        (0, 0): [lambda: own_taper(0)],
        (0, 1): [lambda: own_taper(1)],
        (1, 0): [lambda: cross_taper(0)],
        (1, 1): [lambda: cross_taper(width)],
        (2, 0): [lambda: cross_taper(2 * width)],
        (2, 1): [lambda: cross_taper(3 * width)],
        (3, 0): [lambda: select(0), lambda: select(1)],
        (3, 1): [lambda: select(2), lambda: select(3)],
    }

    def advance(step, m, r):
        centre = e_ref[step, m, r, BASE:BASE + DIRS, :]
        behind = e_ref[step, m, r, BASE - 1:BASE - 1 + DIRS, :]
        ahead = e_ref[step, m, r, BASE + 1:BASE + 1 + DIRS, :]
        if r > 0:
            south = e_ref[step, m, r - 1, BASE:BASE + DIRS, :]
        if r < ROWS - 1:
            north = e_ref[step, m, r + 1, BASE:BASE + DIRS, :]
        if r == 0:
            south = jnp.concatenate([south_ref[step, m] * has_south, north[HALF:]], axis=0)
        if r == ROWS - 1:
            north = jnp.concatenate(
                [south[:16], (north_ref[step, m] * has_north)[:DIRS - 16]], axis=0)
        new = step_row(centre, behind, ahead, jnp.where(pick_y, south, north),
                       cx_ref[r], cy_ref[r], cr_ref[r], pick_x)
        if step < STEPS - 1:
            keep(step + 1, m, r, new)
        else:
            mean_ref[m * ROWS + r:m * ROWS + r + 1, :] = (
                jnp.sum(new, axis=0, keepdims=True) * (1.0 / DIRS))
            send_ref[2 * r, m * DIRS:(m + 1) * DIRS, :] = new[:, :PART]
            send_ref[2 * r + 1, m * DIRS:(m + 1) * DIRS, :] = pltpu.roll(
                new, WIDE - OWN, axis=1)[:, :PART]

    cuts = ((0, 32), (32, 40))

    def part(m, offset):
        to = lax.rem(member + offset, peers)
        first, count = cuts[m]
        return pltpu.make_async_remote_copy(
            src_ref=send_ref.at[to, pl.ds(first, count)],
            dst_ref=state_ref.at[member, pl.ds(first, count)],
            send_sem=part_send.at[m, offset], recv_sem=part_recv.at[m, offset],
            device_id=(space, to), device_id_type=pl.DeviceIdType.MESH)

    order = (4, 3, 5, 2, 6, 1, 7)
    for step in range(STEPS):
        for m in range(2):
            for r in range(1, ROWS - 1):
                advance(step, m, r)
            for work in filler[(step, m)]:
                work()
            halo(step, m, 0).wait_recv()
            advance(step, m, 0)
            if step < STEPS - 1:
                halo(step + 1, m, 1).start()
            halo(step, m, 1).wait_recv()
            advance(step, m, ROWS - 1)
            if step < STEPS - 1:
                halo(step + 1, m, 0).start()
            elif m == 0:
                for offset in order:
                    part(0, offset).start()

    mean = mean_ref[...]
    high = mean.astype(BF16)
    rest = mean - high.astype(F32)
    middle = rest.astype(BF16)
    low = (rest - middle.astype(F32)).astype(BF16)
    slab = (space * ROWS).astype(F32)
    for chunk in range(BATCHES * NOBS // CHUNK):
        batch, part_of = divmod(chunk, NOBS // CHUNK)
        lanes = slice(part_of * CHUNK, (part_of + 1) * CHUNK)
        onehot = onehot_ref[chunk]
        found = (
            jnp.dot(high, onehot, preferred_element_type=F32)
            + jnp.dot(middle, onehot, preferred_element_type=F32)
            + jnp.dot(low, onehot, preferred_element_type=F32))
        row = place_ref[batch:batch + 1, lanes] - slab
        for m in range(2):
            value = jnp.zeros((1, CHUNK), F32)
            for r in range(ROWS):
                value = value + jnp.where(row == float(r), found[m * ROWS + r:m * ROWS + r + 1], 0.0)
            mine_ref[m * 4 + chunk:m * 4 + chunk + 1, :] = value

    def near(index):
        return pltpu.make_async_remote_copy(
            src_ref=mine_ref, dst_ref=near_ref.at[index],
            send_sem=near_send.at[index], recv_sem=near_recv.at[index],
            device_id=(lax.rem(space + shifts[index], spaces), member),
            device_id_type=pl.DeviceIdType.MESH)

    for index in range(4):
        near(index).start()
    own = pltpu.make_async_copy(send_ref.at[member], state_ref.at[member], own_sem)
    own.start()
    for index in range(4):
        near(index).wait_recv()
    sum_ref[...] = mine_ref[...] + near_ref[0] + near_ref[1] + near_ref[2] + near_ref[3]
    block_ref[member] = sum_ref[...]

    def everyone(offset):
        return pltpu.make_async_remote_copy(
            src_ref=sum_ref, dst_ref=block_ref.at[member],
            send_sem=all_send.at[offset], recv_sem=all_recv.at[offset],
            device_id=(space, lax.rem(member + offset, peers)),
            device_id_type=pl.DeviceIdType.MESH)

    for offset in order:
        everyone(offset).start()
    for offset in order:
        part(1, offset).start()
    for offset in order:
        everyone(offset).wait_recv()

    for k in range(MEMBERS):
        for chunk in range(4):
            at = (k % 2) * 4 + chunk
            prior_ref[k:k + 1, chunk * CHUNK:(chunk + 1) * CHUNK] = block_ref[k // 2, at:at + 1, :]
    anomaly, coef = panel(prior_ref[:, :NOBS], value_ref[0:1, :], variance_ref[0:1, :])
    split_mix(anomaly, coef, high_ref, low_ref)
    for at in range(0, NOBS, width):
        gain = mixed(high_ref, low_ref, cross_ref[at:at + width, :])
        prior = prior_ref[:, NOBS + at:NOBS + at + width]
        deviation = prior - jnp.sum(prior, axis=0, keepdims=True) * (1.0 / MEMBERS)
        for l in range(MEMBERS):
            next_ref[l:l + 1, at:at + width] = prior[l:l + 1] + jnp.sum(
                deviation * gain[l * MEMBERS:(l + 1) * MEMBERS], axis=0, keepdims=True)
    gain_ref[0] = mixed(high_ref, low_ref, taper_ref[0]).reshape(MEMBERS, MEMBERS, PART)
    anomaly, coef = panel(next_ref[...], value_ref[1:2, :], variance_ref[1:2, :])
    split_mix(anomaly, coef, high_ref, low_ref)
    gain_ref[1] = mixed(high_ref, low_ref, taper_ref[1]).reshape(MEMBERS, MEMBERS, PART)
    middle_gain = gain_ref[0, 0]
    for l in range(1, MEMBERS):
        middle_gain = middle_gain + gain_ref[0, l]
    middle_gain = middle_gain * (1.0 / MEMBERS)

    def compose(l, carry):
        later = gain_ref[1, l]
        total = gain_ref[0, l] + later
        for k in range(MEMBERS):
            total = total + (gain_ref[0, k] - middle_gain) * later[k:k + 1]
        total_ref[l] = total
        return carry

    lax.fori_loop(0, MEMBERS, compose, 0)

    for step in range(STEPS):
        for m in range(2):
            for side in range(2):
                halo(step, m, side).wait_send()
    own.wait()
    for index in range(4):
        near(index).wait_send()
    for offset in order:
        everyone(offset).wait_send()
    for m in range(2):
        for offset in order:
            part(m, offset).wait()

    for k in range(MEMBERS):
        first = (k % 2) * DIRS
        s_ref[k] = state_ref[k // 2, first:first + DIRS, :]
    centre = s_ref[0]
    for k in range(1, MEMBERS):
        centre = centre + s_ref[k]
    centre = centre * (1.0 / MEMBERS)
    for k in range(MEMBERS):
        s_ref[k] = s_ref[k] - centre
    mean_state = e_ref.at[0, 0, 0, pl.ds(0, DIRS), pl.ds(0, PART)]
    mean_state[...] = centre

    def update(l, carry):
        for tile in range(PART // 128):
            lanes = slice(tile * 128, (tile + 1) * 128)
            total = s_ref[l, :, lanes] + e_ref[0, 0, 0, 0:DIRS, lanes]
            gain = total_ref[l, :, lanes]
            for k in range(MEMBERS):
                total = total + s_ref[k, :, lanes] * gain[k:k + 1]
            count = min(128, OWN - tile * 128)
            out_ref[l, :, tile * 128:tile * 128 + count] = total[:, :count]
        return carry

    lax.fori_loop(0, MEMBERS, update, 0)


def fused(x, speed, turn, trig, cells, values, variances, spaces, peers):
    vmem = pl.BlockSpec(memory_space=pltpu.VMEM)
    dma = pltpu.SemaphoreType.DMA
    return pl.pallas_call(
        functools.partial(wave_kernel, spaces, peers),
        out_shape=jax.ShapeDtypeStruct((MEMBERS, DIRS, OWN), F32),
        in_specs=[vmem] * 7,
        out_specs=vmem,
        scratch_shapes=[
            pltpu.VMEM((STEPS, 2, ROWS, TALL, WIDE), F32),
            pltpu.VMEM((STEPS, 2, HALF, WIDE), F32),
            pltpu.VMEM((STEPS, 2, HALF, WIDE), F32),
            pltpu.VMEM((ROWS, DIRS, WIDE), F32),
            pltpu.VMEM((ROWS, DIRS, WIDE), F32),
            pltpu.VMEM((ROWS, DIRS, WIDE), F32),
            pltpu.VMEM((2 * ROWS, 2 * DIRS, PART), F32),
            pltpu.VMEM((2 * ROWS, WIDE), F32),
            pltpu.VMEM((8, CHUNK), F32),
            pltpu.VMEM((4, 8, CHUNK), F32),
            pltpu.VMEM((8, CHUNK), F32),
            pltpu.VMEM((peers, 2 * DIRS, PART), F32),
            pltpu.VMEM((peers, 8, CHUNK), F32),
            pltpu.VMEM((8, NOBS), F32),
            pltpu.VMEM((NOBS, 8), F32),
            pltpu.VMEM((NOBS, NOBS), BF16),
            pltpu.VMEM((BATCHES, PART, NOBS), BF16),
            pltpu.VMEM((BATCHES * NOBS // CHUNK, WIDE, CHUNK), BF16),
            pltpu.VMEM((MEMBERS, DIRS, PART), F32),
            pltpu.VMEM((MEMBERS, BATCHES * NOBS), F32),
            pltpu.VMEM((MEMBERS, NOBS), F32),
            pltpu.VMEM((MEMBERS * MEMBERS, NOBS), BF16),
            pltpu.VMEM((MEMBERS * MEMBERS, NOBS), BF16),
            pltpu.VMEM((BATCHES, MEMBERS, MEMBERS, PART), F32),
            pltpu.VMEM((MEMBERS, MEMBERS, PART), F32),
            dma((STEPS, 2, 2)), dma((STEPS, 2, 2)),
            dma((2, 8)), dma((2, 8)),
            dma((4,)), dma((4,)),
            dma((8,)), dma((8,)),
            dma(()),
        ],
        compiler_params=pltpu.CompilerParams(collective_id=0, has_side_effects=True),
        name="fused",
    )(x, speed, turn, trig, cells, values, variances)


def per_device(spectra, group_speed, turning_rate, obs_cell, obs_value, obs_variance):
    spaces, peers = lax.axis_size("space"), lax.axis_size("member")
    angles = (2.0 * math.pi * np.arange(DIRS, dtype=np.float32) / DIRS).astype(np.float32)
    trig = np.stack([np.cos(angles), np.sin(angles)]).astype(np.float32)
    trig = np.ascontiguousarray(np.broadcast_to(trig[:, :, None], (2, DIRS, 128)))
    x = jnp.transpose(spectra, (0, 2, 1, 3))
    return fused(x, group_speed, turning_rate, jnp.asarray(trig), obs_cell, obs_value,
                 obs_variance, spaces, peers)


def solution(mesh):
    placed = (P("member", None, "space", None), P("space", None), P("space", None), P(), P(), P())
    return jax.shard_map(
        per_device,
        mesh=mesh,
        in_specs=placed,
        out_specs=P(None, None, ("space", "member")),
        check_vma=False,
    )
```

```python
import functools
import math

import jax
import jax.numpy as jnp
import numpy as np
from jax import lax
from jax.experimental import pallas as pl
from jax.experimental.pallas import tpu as pltpu
from jax.sharding import PartitionSpec as P

LON = 720
STEPS = 4
BATCHES = 2
LOC = 4
DIRS = 36
NOBS = 1024
MEMBERS = 16
ROWS = 4
OWN = 360
WIDE = 768
TALL = 48
BASE = 8
PART = 384
HALF = 24
CHUNK = 512
F32 = jnp.float32
BF16 = jnp.bfloat16


def step_row(centre, behind, ahead, upwind_y, cx, cy, cr, pick_x):
    west = pltpu.roll(centre, 1, axis=1)
    east = pltpu.roll(centre, WIDE - 1, axis=1)
    result = centre - cx * (centre - jnp.where(pick_x, west, east))
    result = result - cy * (centre - upwind_y)
    return result - jnp.abs(cr) * (centre - jnp.where(cr > 0.0, behind, ahead))


def widen(array):
    return jnp.concatenate([array, array[:, :24], array[:, LON - 24:]], axis=1)


def panel(prior, values, variance):
    centre = jnp.sum(prior, axis=0, keepdims=True) * (1.0 / MEMBERS)
    anomaly = prior - centre
    spread = jnp.sum(anomaly * anomaly, axis=0, keepdims=True) * (1.0 / (MEMBERS - 1))
    total = spread + variance
    shrink = 1.0 / (1.0 + jnp.sqrt(variance / total))
    coef = ((values - centre) - shrink * anomaly) / (total * (MEMBERS - 1))
    return anomaly, coef


def split_mix(anomaly, coef, high_ref, low_ref):
    for l in range(MEMBERS):
        mix = anomaly * coef[l:l + 1]
        high = mix.astype(BF16)
        high_ref[l * MEMBERS:(l + 1) * MEMBERS, :] = high
        low_ref[l * MEMBERS:(l + 1) * MEMBERS, :] = (mix - high.astype(F32)).astype(BF16)


def taper(row, lon, rows, lons):
    lat_gap = row - rows
    lon_gap = jnp.abs(lon - lons)
    lon_gap = jnp.minimum(lon_gap, LON - lon_gap)
    near = jnp.maximum(1.0 - (lat_gap * lat_gap + lon_gap * lon_gap) * (1.0 / (LOC * LOC)), 0.0)
    return (near * near).astype(BF16)


def mixed(high_ref, low_ref, weights):
    dims = (((1,), (1,)), ((), ()))
    return lax.dot_general(
        high_ref[...], weights, dims, preferred_element_type=F32
    ) + lax.dot_general(low_ref[...], weights, dims, preferred_element_type=F32)


def wave_kernel(
    spaces, peers,
    x_ref, speed_ref, turn_ref, trig_ref, cell_ref, value_ref, variance_ref,
    out_ref,
    e_ref, south_ref, north_ref, cx_ref, cy_ref, cr_ref, send_ref, mean_ref,
    mine_ref, near_ref, sum_ref, state_ref, block_ref, place_ref, column_ref,
    cross_ref, taper_ref, onehot_ref, s_ref, prior_ref, next_ref,
    high_ref, low_ref, gain_ref, total_ref,
    halo_send, halo_recv, part_send, part_recv, near_send, near_recv,
    all_send, all_recv, own_sem, relay_ref, relay_send, relay_recv,
):
    space = lax.axis_index("space")
    member = lax.axis_index("member")
    shifts = (1, spaces - 1, 2, spaces - 2)

    barrier = pltpu.get_barrier_semaphore()
    for shift in shifts:
        pl.semaphore_signal(
            barrier, inc=1, device_id=(lax.rem(space + shift, spaces), member),
            device_id_type=pl.DeviceIdType.MESH)
    for offset in range(1, peers):
        pl.semaphore_signal(
            barrier, inc=1, device_id=(space, lax.rem(member + offset, peers)),
            device_id_type=pl.DeviceIdType.MESH)

    def keep(step, m, r, new):
        e_ref[step, m, r, BASE:BASE + DIRS, :] = new
        e_ref[step, m, r, BASE - 1:BASE, :] = new[DIRS - 1:DIRS]
        e_ref[step, m, r, BASE + DIRS:BASE + DIRS + 1, :] = new[0:1]

    for r in (0, ROWS - 1, 1, 2):
        for m in range(2):
            keep(0, m, r, widen(x_ref[m, :, r, :]))
    pl.semaphore_wait(barrier, len(shifts) + peers - 1)

    def halo(step, m, side):
        if side == 0:
            source = e_ref.at[step, m, ROWS - 1, pl.ds(BASE, HALF)]
            target, to = south_ref.at[step, m], lax.rem(space + 1, spaces)
        else:
            source = e_ref.at[step, m, 0, pl.ds(BASE + 16, HALF)]
            target, to = north_ref.at[step, m], lax.rem(space + spaces - 1, spaces)
        return pltpu.make_async_remote_copy(
            src_ref=source, dst_ref=target,
            send_sem=halo_send.at[step, m, side], recv_sem=halo_recv.at[step, m, side],
            device_id=(to, member), device_id_type=pl.DeviceIdType.MESH)

    for m in range(2):
        for side in range(2):
            halo(0, m, side).start()

    cosines = jnp.concatenate([trig_ref[0]] * (WIDE // 128), axis=1)
    sines = jnp.concatenate([trig_ref[1]] * (WIDE // 128), axis=1)
    speeds = widen(speed_ref[...])
    turns = widen(turn_ref[...])
    for r in range(ROWS):
        cx_ref[r] = speeds[r:r + 1, :] * jnp.abs(cosines)
        cy_ref[r] = speeds[r:r + 1, :] * jnp.abs(sines)
        cr_ref[r] = turns[r:r + 1, :] * cosines
    pick_x = cosines > 0.0
    pick_y = sines > 0.0
    has_south = (space > 0).astype(F32)
    has_north = (space < spaces - 1).astype(F32)

    cells = cell_ref[...].astype(F32)
    rows = jnp.floor((cells + 0.5) * (1.0 / LON))
    lons = cells - rows * float(LON)
    place_ref[...] = jnp.concatenate([rows, lons, rows, lons], axis=0)
    column_ref[...] = jnp.transpose(place_ref[...])

    device = space * peers + member
    own_row = (device // 2).astype(F32)
    own_lon = ((device % 2) * OWN).astype(F32)

    def own_taper(batch):
        cell_lon = lax.broadcasted_iota(jnp.int32, (PART, 128), 0).astype(F32) + own_lon
        cell_lon = jnp.concatenate([cell_lon] * (NOBS // 128), axis=1)
        taper_ref[batch] = taper(own_row, cell_lon, place_ref[batch:batch + 1, :],
                                 place_ref[2 + batch:3 + batch, :])

    width = 256

    def cross_taper(at):
        cross_ref[at:at + width, :] = taper(
            column_ref[at:at + width, 1:2], column_ref[at:at + width, 3:4],
            place_ref[0:1, :], place_ref[2:3, :])

    def select(chunk):
        batch, part_of = divmod(chunk, NOBS // CHUNK)
        lanes = slice(part_of * CHUNK, (part_of + 1) * CHUNK)
        where_lon = lax.broadcasted_iota(jnp.int32, (WIDE, CHUNK), 0).astype(F32)
        onehot_ref[chunk] = jnp.where(
            where_lon == place_ref[2 + batch:3 + batch, lanes], 1.0, 0.0).astype(BF16)

    filler = {
        (0, 0): [lambda: own_taper(0)],
        (0, 1): [lambda: own_taper(1)],
        (1, 0): [lambda: cross_taper(0)],
        (1, 1): [lambda: cross_taper(width)],
        (2, 0): [lambda: cross_taper(2 * width)],
        (2, 1): [lambda: cross_taper(3 * width)],
        (3, 0): [lambda: select(0), lambda: select(1)],
        (3, 1): [lambda: select(2), lambda: select(3)],
    }

    def advance(step, m, r):
        centre = e_ref[step, m, r, BASE:BASE + DIRS, :]
        behind = e_ref[step, m, r, BASE - 1:BASE - 1 + DIRS, :]
        ahead = e_ref[step, m, r, BASE + 1:BASE + 1 + DIRS, :]
        if r > 0:
            south = e_ref[step, m, r - 1, BASE:BASE + DIRS, :]
        if r < ROWS - 1:
            north = e_ref[step, m, r + 1, BASE:BASE + DIRS, :]
        if r == 0:
            south = jnp.concatenate([south_ref[step, m] * has_south, north[HALF:]], axis=0)
        if r == ROWS - 1:
            north = jnp.concatenate(
                [south[:16], (north_ref[step, m] * has_north)[:DIRS - 16]], axis=0)
        new = step_row(centre, behind, ahead, jnp.where(pick_y, south, north),
                       cx_ref[r], cy_ref[r], cr_ref[r], pick_x)
        if step < STEPS - 1:
            keep(step + 1, m, r, new)
        else:
            mean_ref[m * ROWS + r:m * ROWS + r + 1, :] = (
                jnp.sum(new, axis=0, keepdims=True) * (1.0 / DIRS))
            send_ref[2 * r, m * DIRS:(m + 1) * DIRS, :] = new[:, :PART]
            send_ref[2 * r + 1, m * DIRS:(m + 1) * DIRS, :] = pltpu.roll(
                new, WIDE - OWN, axis=1)[:, :PART]

    cuts = ((0, 32), (32, 40))

    chips = peers // 2
    chip, core = member // 2, lax.rem(member, 2)

    def peer(away, other):
        return 2 * lax.rem(chip + away + chips, chips) + (lax.rem(core + 1, 2) if other else core)

    def part(m, index):
        away, other = divmod(index, 2)
        to = peer(away, other)
        first, count = cuts[m]
        return pltpu.make_async_remote_copy(
            src_ref=send_ref.at[to, pl.ds(first, count)],
            dst_ref=state_ref.at[member, pl.ds(first, count)],
            send_sem=part_send.at[m, index], recv_sem=part_recv.at[m, index],
            device_id=(space, to), device_id_type=pl.DeviceIdType.MESH)

    def relay(m, other):
        first, count = cuts[m]
        return pltpu.make_async_remote_copy(
            src_ref=send_ref.at[peer(2, other), pl.ds(first, count)],
            dst_ref=relay_ref.at[m, other, pl.ds(0, count)],
            send_sem=relay_send.at[m, other], recv_sem=relay_recv.at[m, other],
            device_id=(space, peer(-1 if other else 1, False)),
            device_id_type=pl.DeviceIdType.MESH)

    def forward(m, other):
        first, count = cuts[m]
        step = -1 if other else 1
        return pltpu.make_async_remote_copy(
            src_ref=relay_ref.at[m, other, pl.ds(0, count)],
            dst_ref=state_ref.at[peer(-step, False), pl.ds(first, count)],
            send_sem=part_send.at[m, 4 + other], recv_sem=part_recv.at[m, 4 + other],
            device_id=(space, peer(step, other)),
            device_id_type=pl.DeviceIdType.MESH)

    def scatter(m):
        for other in range(2):
            relay(m, other).start()
        for index in (2, 6, 3, 7, 1):
            part(m, index).start()

    def pass_on(m):
        for other in range(2):
            relay(m, other).wait_recv()
            forward(m, other).start()

    order = (4, 3, 5, 2, 6, 1, 7)
    for step in range(STEPS):
        for m in range(2):
            for r in range(1, ROWS - 1):
                advance(step, m, r)
            for work in filler[(step, m)]:
                work()
            halo(step, m, 0).wait_recv()
            advance(step, m, 0)
            if step < STEPS - 1:
                halo(step + 1, m, 1).start()
            halo(step, m, 1).wait_recv()
            advance(step, m, ROWS - 1)
            if step < STEPS - 1:
                halo(step + 1, m, 0).start()
            elif m == 0:
                scatter(0)

    mean = mean_ref[...]
    high = mean.astype(BF16)
    rest = mean - high.astype(F32)
    middle = rest.astype(BF16)
    low = (rest - middle.astype(F32)).astype(BF16)
    slab = (space * ROWS).astype(F32)
    for chunk in range(BATCHES * NOBS // CHUNK):
        batch, part_of = divmod(chunk, NOBS // CHUNK)
        lanes = slice(part_of * CHUNK, (part_of + 1) * CHUNK)
        onehot = onehot_ref[chunk]
        found = (
            jnp.dot(high, onehot, preferred_element_type=F32)
            + jnp.dot(middle, onehot, preferred_element_type=F32)
            + jnp.dot(low, onehot, preferred_element_type=F32))
        row = place_ref[batch:batch + 1, lanes] - slab
        for m in range(2):
            value = jnp.zeros((1, CHUNK), F32)
            for r in range(ROWS):
                value = value + jnp.where(row == float(r), found[m * ROWS + r:m * ROWS + r + 1], 0.0)
            mine_ref[m * 4 + chunk:m * 4 + chunk + 1, :] = value

    def near(index):
        return pltpu.make_async_remote_copy(
            src_ref=mine_ref, dst_ref=near_ref.at[index],
            send_sem=near_send.at[index], recv_sem=near_recv.at[index],
            device_id=(lax.rem(space + shifts[index], spaces), member),
            device_id_type=pl.DeviceIdType.MESH)

    for index in range(4):
        near(index).start()
    own = pltpu.make_async_copy(send_ref.at[member], state_ref.at[member], own_sem)
    own.start()
    for index in range(4):
        near(index).wait_recv()
    sum_ref[...] = mine_ref[...] + near_ref[0] + near_ref[1] + near_ref[2] + near_ref[3]
    block_ref[member] = sum_ref[...]

    def everyone(offset):
        return pltpu.make_async_remote_copy(
            src_ref=sum_ref, dst_ref=block_ref.at[member],
            send_sem=all_send.at[offset], recv_sem=all_recv.at[offset],
            device_id=(space, lax.rem(member + offset, peers)),
            device_id_type=pl.DeviceIdType.MESH)

    for offset in order:
        everyone(offset).start()
    pass_on(0)
    scatter(1)
    for offset in order:
        everyone(offset).wait_recv()
    pass_on(1)

    for k in range(MEMBERS):
        for chunk in range(4):
            at = (k % 2) * 4 + chunk
            prior_ref[k:k + 1, chunk * CHUNK:(chunk + 1) * CHUNK] = block_ref[k // 2, at:at + 1, :]
    anomaly, coef = panel(prior_ref[:, :NOBS], value_ref[0:1, :], variance_ref[0:1, :])
    split_mix(anomaly, coef, high_ref, low_ref)
    for at in range(0, NOBS, width):
        gain = mixed(high_ref, low_ref, cross_ref[at:at + width, :])
        prior = prior_ref[:, NOBS + at:NOBS + at + width]
        deviation = prior - jnp.sum(prior, axis=0, keepdims=True) * (1.0 / MEMBERS)
        for l in range(MEMBERS):
            next_ref[l:l + 1, at:at + width] = prior[l:l + 1] + jnp.sum(
                deviation * gain[l * MEMBERS:(l + 1) * MEMBERS], axis=0, keepdims=True)
    gain_ref[0] = mixed(high_ref, low_ref, taper_ref[0]).reshape(MEMBERS, MEMBERS, PART)
    anomaly, coef = panel(next_ref[...], value_ref[1:2, :], variance_ref[1:2, :])
    split_mix(anomaly, coef, high_ref, low_ref)
    gain_ref[1] = mixed(high_ref, low_ref, taper_ref[1]).reshape(MEMBERS, MEMBERS, PART)
    middle_gain = gain_ref[0, 0]
    for l in range(1, MEMBERS):
        middle_gain = middle_gain + gain_ref[0, l]
    middle_gain = middle_gain * (1.0 / MEMBERS)

    def compose(l, carry):
        later = gain_ref[1, l]
        total = gain_ref[0, l] + later
        for k in range(MEMBERS):
            total = total + (gain_ref[0, k] - middle_gain) * later[k:k + 1]
        total_ref[l] = total
        return carry

    lax.fori_loop(0, MEMBERS, compose, 0)

    for step in range(STEPS):
        for m in range(2):
            for side in range(2):
                halo(step, m, side).wait_send()
    own.wait()
    for index in range(4):
        near(index).wait_send()
    for offset in order:
        everyone(offset).wait_send()
    for m in range(2):
        for index in (1, 2, 3, 6, 7):
            part(m, index).wait()
        for other in range(2):
            relay(m, other).wait_send()
            forward(m, other).wait()

    for k in range(MEMBERS):
        first = (k % 2) * DIRS
        s_ref[k] = state_ref[k // 2, first:first + DIRS, :]
    centre = s_ref[0]
    for k in range(1, MEMBERS):
        centre = centre + s_ref[k]
    centre = centre * (1.0 / MEMBERS)
    for k in range(MEMBERS):
        s_ref[k] = s_ref[k] - centre
    mean_state = e_ref.at[0, 0, 0, pl.ds(0, DIRS), pl.ds(0, PART)]
    mean_state[...] = centre

    def update(l, carry):
        for tile in range(PART // 128):
            lanes = slice(tile * 128, (tile + 1) * 128)
            total = s_ref[l, :, lanes] + e_ref[0, 0, 0, 0:DIRS, lanes]
            gain = total_ref[l, :, lanes]
            for k in range(MEMBERS):
                total = total + s_ref[k, :, lanes] * gain[k:k + 1]
            count = min(128, OWN - tile * 128)
            out_ref[l, :, tile * 128:tile * 128 + count] = total[:, :count]
        return carry

    lax.fori_loop(0, MEMBERS, update, 0)


def fused(x, speed, turn, trig, cells, values, variances, spaces, peers):
    vmem = pl.BlockSpec(memory_space=pltpu.VMEM)
    dma = pltpu.SemaphoreType.DMA
    return pl.pallas_call(
        functools.partial(wave_kernel, spaces, peers),
        out_shape=jax.ShapeDtypeStruct((MEMBERS, DIRS, OWN), F32),
        in_specs=[vmem] * 7,
        out_specs=vmem,
        scratch_shapes=[
            pltpu.VMEM((STEPS, 2, ROWS, TALL, WIDE), F32),
            pltpu.VMEM((STEPS, 2, HALF, WIDE), F32),
            pltpu.VMEM((STEPS, 2, HALF, WIDE), F32),
            pltpu.VMEM((ROWS, DIRS, WIDE), F32),
            pltpu.VMEM((ROWS, DIRS, WIDE), F32),
            pltpu.VMEM((ROWS, DIRS, WIDE), F32),
            pltpu.VMEM((2 * ROWS, 2 * DIRS, PART), F32),
            pltpu.VMEM((2 * ROWS, WIDE), F32),
            pltpu.VMEM((8, CHUNK), F32),
            pltpu.VMEM((4, 8, CHUNK), F32),
            pltpu.VMEM((8, CHUNK), F32),
            pltpu.VMEM((peers, 2 * DIRS, PART), F32),
            pltpu.VMEM((peers, 8, CHUNK), F32),
            pltpu.VMEM((8, NOBS), F32),
            pltpu.VMEM((NOBS, 8), F32),
            pltpu.VMEM((NOBS, NOBS), BF16),
            pltpu.VMEM((BATCHES, PART, NOBS), BF16),
            pltpu.VMEM((BATCHES * NOBS // CHUNK, WIDE, CHUNK), BF16),
            pltpu.VMEM((MEMBERS, DIRS, PART), F32),
            pltpu.VMEM((MEMBERS, BATCHES * NOBS), F32),
            pltpu.VMEM((MEMBERS, NOBS), F32),
            pltpu.VMEM((MEMBERS * MEMBERS, NOBS), BF16),
            pltpu.VMEM((MEMBERS * MEMBERS, NOBS), BF16),
            pltpu.VMEM((BATCHES, MEMBERS, MEMBERS, PART), F32),
            pltpu.VMEM((MEMBERS, MEMBERS, PART), F32),
            dma((STEPS, 2, 2)), dma((STEPS, 2, 2)),
            dma((2, 8)), dma((2, 8)),
            dma((4,)), dma((4,)),
            dma((8,)), dma((8,)),
            dma(()),
            pltpu.VMEM((2, 2, 40, PART), F32),
            dma((2, 2)), dma((2, 2)),
        ],
        compiler_params=pltpu.CompilerParams(collective_id=0, has_side_effects=True),
        name="fused",
    )(x, speed, turn, trig, cells, values, variances)


def per_device(spectra, group_speed, turning_rate, obs_cell, obs_value, obs_variance):
    spaces, peers = lax.axis_size("space"), lax.axis_size("member")
    angles = (2.0 * math.pi * np.arange(DIRS, dtype=np.float32) / DIRS).astype(np.float32)
    trig = np.stack([np.cos(angles), np.sin(angles)]).astype(np.float32)
    trig = np.ascontiguousarray(np.broadcast_to(trig[:, :, None], (2, DIRS, 128)))
    return fused(spectra, group_speed, turning_rate, jnp.asarray(trig), obs_cell, obs_value,
                 obs_variance, spaces, peers)


def solution(mesh):
    placed = (P("member", None, "space", None), P("space", None), P("space", None), P(), P(), P())
    return jax.shard_map(
        per_device,
        mesh=mesh,
        in_specs=placed,
        out_specs=P(None, None, ("space", "member")),
        check_vma=False,
    )
```

```python
import functools
import math

import jax
import jax.numpy as jnp
import numpy as np
from jax import lax
from jax.experimental import pallas as pl
from jax.experimental.pallas import tpu as pltpu
from jax.sharding import PartitionSpec as P

LON = 720
STEPS = 4
BATCHES = 2
LOC = 4
DIRS = 36
NOBS = 1024
MEMBERS = 16
ROWS = 4
OWN = 360
WIDE = 768
TALL = 48
BASE = 8
PART = 384
HALF = 24
CHUNK = 512
F32 = jnp.float32
BF16 = jnp.bfloat16


def step_row(centre, behind, ahead, upwind_y, cx, cy, cr, pick_x):
    west = pltpu.roll(centre, 1, axis=1)
    east = pltpu.roll(centre, WIDE - 1, axis=1)
    result = centre - cx * (centre - jnp.where(pick_x, west, east))
    result = result - cy * (centre - upwind_y)
    return result - jnp.abs(cr) * (centre - jnp.where(cr > 0.0, behind, ahead))


def widen(array):
    return jnp.concatenate([array, array[:, :24], array[:, LON - 24:]], axis=1)


def panel(prior, values, variance):
    centre = jnp.sum(prior, axis=0, keepdims=True) * (1.0 / MEMBERS)
    anomaly = prior - centre
    spread = jnp.sum(anomaly * anomaly, axis=0, keepdims=True) * (1.0 / (MEMBERS - 1))
    total = spread + variance
    shrink = 1.0 / (1.0 + jnp.sqrt(variance / total))
    coef = ((values - centre) - shrink * anomaly) / (total * (MEMBERS - 1))
    return anomaly, coef


def split_mix(anomaly, coef, high_ref, low_ref):
    for l in range(MEMBERS):
        mix = anomaly * coef[l:l + 1]
        high = mix.astype(BF16)
        high_ref[l * MEMBERS:(l + 1) * MEMBERS, :] = high
        low_ref[l * MEMBERS:(l + 1) * MEMBERS, :] = (mix - high.astype(F32)).astype(BF16)


def taper(row, lon, rows, lons):
    lat_gap = row - rows
    lon_gap = jnp.abs(lon - lons)
    lon_gap = jnp.minimum(lon_gap, LON - lon_gap)
    near = jnp.maximum(1.0 - (lat_gap * lat_gap + lon_gap * lon_gap) * (1.0 / (LOC * LOC)), 0.0)
    return (near * near).astype(BF16)


def mixed(high_ref, low_ref, weights):
    dims = (((1,), (1,)), ((), ()))
    return lax.dot_general(
        high_ref[...], weights, dims, preferred_element_type=F32
    ) + lax.dot_general(low_ref[...], weights, dims, preferred_element_type=F32)


def wave_kernel(
    spaces, peers,
    x_ref, speed_ref, turn_ref, trig_ref, cell_ref, value_ref, variance_ref,
    out_ref,
    e_ref, south_ref, north_ref, cx_ref, cy_ref, cr_ref, send_ref, mean_ref,
    mine_ref, near_ref, sum_ref, state_ref, block_ref, place_ref, column_ref,
    cross_ref, taper_ref, onehot_ref, s_ref, prior_ref, next_ref,
    high_ref, low_ref, gain_ref, total_ref,
    halo_send, halo_recv, part_send, part_recv, near_send, near_recv,
    all_send, all_recv, own_sem,
):
    space = lax.axis_index("space")
    member = lax.axis_index("member")
    shifts = (1, spaces - 1, 2, spaces - 2)

    barrier = pltpu.get_barrier_semaphore()
    for shift in shifts:
        pl.semaphore_signal(
            barrier, inc=1, device_id=(lax.rem(space + shift, spaces), member),
            device_id_type=pl.DeviceIdType.MESH)
    for offset in range(1, peers):
        pl.semaphore_signal(
            barrier, inc=1, device_id=(space, lax.rem(member + offset, peers)),
            device_id_type=pl.DeviceIdType.MESH)

    def keep(step, m, r, new):
        e_ref[step, m, r, BASE:BASE + DIRS, :] = new
        e_ref[step, m, r, BASE - 1:BASE, :] = new[DIRS - 1:DIRS]
        e_ref[step, m, r, BASE + DIRS:BASE + DIRS + 1, :] = new[0:1]

    for r in (0, ROWS - 1, 1, 2):
        for m in range(2):
            keep(0, m, r, widen(x_ref[m, :, r, :]))
    pl.semaphore_wait(barrier, len(shifts) + peers - 1)

    def halo(step, m, side):
        if side == 0:
            source = e_ref.at[step, m, ROWS - 1, pl.ds(BASE, HALF)]
            target, to = south_ref.at[step, m], lax.rem(space + 1, spaces)
        else:
            source = e_ref.at[step, m, 0, pl.ds(BASE + 16, HALF)]
            target, to = north_ref.at[step, m], lax.rem(space + spaces - 1, spaces)
        return pltpu.make_async_remote_copy(
            src_ref=source, dst_ref=target,
            send_sem=halo_send.at[step, m, side], recv_sem=halo_recv.at[step, m, side],
            device_id=(to, member), device_id_type=pl.DeviceIdType.MESH)

    for m in range(2):
        for side in range(2):
            halo(0, m, side).start()

    cosines = jnp.concatenate([trig_ref[0]] * (WIDE // 128), axis=1)
    sines = jnp.concatenate([trig_ref[1]] * (WIDE // 128), axis=1)
    speeds = widen(speed_ref[...])
    turns = widen(turn_ref[...])
    for r in range(ROWS):
        cx_ref[r] = speeds[r:r + 1, :] * jnp.abs(cosines)
        cy_ref[r] = speeds[r:r + 1, :] * jnp.abs(sines)
        cr_ref[r] = turns[r:r + 1, :] * cosines
    pick_x = cosines > 0.0
    pick_y = sines > 0.0
    has_south = (space > 0).astype(F32)
    has_north = (space < spaces - 1).astype(F32)

    cells = cell_ref[...].astype(F32)
    rows = jnp.floor((cells + 0.5) * (1.0 / LON))
    lons = cells - rows * float(LON)
    place_ref[...] = jnp.concatenate([rows, lons, rows, lons], axis=0)
    column_ref[...] = jnp.transpose(place_ref[...])

    device = space * peers + member
    own_row = (device // 2).astype(F32)
    own_lon = ((device % 2) * OWN).astype(F32)

    def own_taper(batch):
        cell_lon = lax.broadcasted_iota(jnp.int32, (PART, 128), 0).astype(F32) + own_lon
        cell_lon = jnp.concatenate([cell_lon] * (NOBS // 128), axis=1)
        taper_ref[batch] = taper(own_row, cell_lon, place_ref[batch:batch + 1, :],
                                 place_ref[2 + batch:3 + batch, :])

    width = 256

    def cross_taper(at):
        cross_ref[at:at + width, :] = taper(
            column_ref[at:at + width, 1:2], column_ref[at:at + width, 3:4],
            place_ref[0:1, :], place_ref[2:3, :])

    def select(chunk):
        batch, part_of = divmod(chunk, NOBS // CHUNK)
        lanes = slice(part_of * CHUNK, (part_of + 1) * CHUNK)
        where_lon = lax.broadcasted_iota(jnp.int32, (WIDE, CHUNK), 0).astype(F32)
        onehot_ref[chunk] = jnp.where(
            where_lon == place_ref[2 + batch:3 + batch, lanes], 1.0, 0.0).astype(BF16)

    filler = {
        (0, 0): [lambda: own_taper(0)],
        (0, 1): [lambda: own_taper(1)],
        (1, 0): [lambda: cross_taper(0)],
        (1, 1): [lambda: cross_taper(width)],
        (2, 0): [lambda: cross_taper(2 * width)],
        (2, 1): [lambda: cross_taper(3 * width)],
        (3, 0): [lambda: select(0), lambda: select(1)],
        (3, 1): [lambda: select(2), lambda: select(3)],
    }

    def advance(step, m, r):
        centre = e_ref[step, m, r, BASE:BASE + DIRS, :]
        behind = e_ref[step, m, r, BASE - 1:BASE - 1 + DIRS, :]
        ahead = e_ref[step, m, r, BASE + 1:BASE + 1 + DIRS, :]
        if r > 0:
            south = e_ref[step, m, r - 1, BASE:BASE + DIRS, :]
        if r < ROWS - 1:
            north = e_ref[step, m, r + 1, BASE:BASE + DIRS, :]
        if r == 0:
            south = jnp.concatenate([south_ref[step, m] * has_south, north[HALF:]], axis=0)
        if r == ROWS - 1:
            north = jnp.concatenate(
                [south[:16], (north_ref[step, m] * has_north)[:DIRS - 16]], axis=0)
        new = step_row(centre, behind, ahead, jnp.where(pick_y, south, north),
                       cx_ref[r], cy_ref[r], cr_ref[r], pick_x)
        if step < STEPS - 1:
            keep(step + 1, m, r, new)
        else:
            mean_ref[m * ROWS + r:m * ROWS + r + 1, :] = (
                jnp.sum(new, axis=0, keepdims=True) * (1.0 / DIRS))
            send_ref[2 * r, m * DIRS:(m + 1) * DIRS, :] = new[:, :PART]
            send_ref[2 * r + 1, m * DIRS:(m + 1) * DIRS, :] = pltpu.roll(
                new, WIDE - OWN, axis=1)[:, :PART]

    cuts = ((0, 32), (32, 40))

    def part(m, offset):
        to = lax.rem(member + offset, peers)
        first, count = cuts[m]
        return pltpu.make_async_remote_copy(
            src_ref=send_ref.at[to, pl.ds(first, count)],
            dst_ref=state_ref.at[member, pl.ds(first, count)],
            send_sem=part_send.at[m, offset], recv_sem=part_recv.at[m, offset],
            device_id=(space, to), device_id_type=pl.DeviceIdType.MESH)

    order = (4, 3, 5, 2, 6, 1, 7)
    for step in range(STEPS):
        for m in range(2):
            for r in range(1, ROWS - 1):
                advance(step, m, r)
            for work in filler[(step, m)]:
                work()
            halo(step, m, 0).wait_recv()
            advance(step, m, 0)
            if step < STEPS - 1:
                halo(step + 1, m, 1).start()
            halo(step, m, 1).wait_recv()
            advance(step, m, ROWS - 1)
            if step < STEPS - 1:
                halo(step + 1, m, 0).start()
            elif m == 0:
                for offset in order:
                    part(0, offset).start()

    mean = mean_ref[...]
    high = mean.astype(BF16)
    rest = mean - high.astype(F32)
    middle = rest.astype(BF16)
    low = (rest - middle.astype(F32)).astype(BF16)
    slab = (space * ROWS).astype(F32)
    for chunk in range(BATCHES * NOBS // CHUNK):
        batch, part_of = divmod(chunk, NOBS // CHUNK)
        lanes = slice(part_of * CHUNK, (part_of + 1) * CHUNK)
        onehot = onehot_ref[chunk]
        found = (
            jnp.dot(high, onehot, preferred_element_type=F32)
            + jnp.dot(middle, onehot, preferred_element_type=F32)
            + jnp.dot(low, onehot, preferred_element_type=F32))
        row = place_ref[batch:batch + 1, lanes] - slab
        for m in range(2):
            value = jnp.zeros((1, CHUNK), F32)
            for r in range(ROWS):
                value = value + jnp.where(row == float(r), found[m * ROWS + r:m * ROWS + r + 1], 0.0)
            mine_ref[m * 4 + chunk:m * 4 + chunk + 1, :] = value

    def near(index):
        return pltpu.make_async_remote_copy(
            src_ref=mine_ref, dst_ref=near_ref.at[index],
            send_sem=near_send.at[index], recv_sem=near_recv.at[index],
            device_id=(lax.rem(space + shifts[index], spaces), member),
            device_id_type=pl.DeviceIdType.MESH)

    for index in range(4):
        near(index).start()
    own = pltpu.make_async_copy(send_ref.at[member], state_ref.at[member], own_sem)
    own.start()
    for index in range(4):
        near(index).wait_recv()
    sum_ref[...] = mine_ref[...] + near_ref[0] + near_ref[1] + near_ref[2] + near_ref[3]
    block_ref[member] = sum_ref[...]

    def everyone(offset):
        return pltpu.make_async_remote_copy(
            src_ref=sum_ref, dst_ref=block_ref.at[member],
            send_sem=all_send.at[offset], recv_sem=all_recv.at[offset],
            device_id=(space, lax.rem(member + offset, peers)),
            device_id_type=pl.DeviceIdType.MESH)

    for offset in order:
        everyone(offset).start()
    for offset in order:
        part(1, offset).start()
    for offset in order:
        everyone(offset).wait_recv()

    for k in range(MEMBERS):
        for chunk in range(4):
            at = (k % 2) * 4 + chunk
            prior_ref[k:k + 1, chunk * CHUNK:(chunk + 1) * CHUNK] = block_ref[k // 2, at:at + 1, :]
    anomaly, coef = panel(prior_ref[:, :NOBS], value_ref[0:1, :], variance_ref[0:1, :])
    split_mix(anomaly, coef, high_ref, low_ref)
    for at in range(0, NOBS, width):
        gain = mixed(high_ref, low_ref, cross_ref[at:at + width, :])
        prior = prior_ref[:, NOBS + at:NOBS + at + width]
        deviation = prior - jnp.sum(prior, axis=0, keepdims=True) * (1.0 / MEMBERS)
        for l in range(MEMBERS):
            next_ref[l:l + 1, at:at + width] = prior[l:l + 1] + jnp.sum(
                deviation * gain[l * MEMBERS:(l + 1) * MEMBERS], axis=0, keepdims=True)
    gain_ref[0] = mixed(high_ref, low_ref, taper_ref[0]).reshape(MEMBERS, MEMBERS, PART)
    anomaly, coef = panel(next_ref[...], value_ref[1:2, :], variance_ref[1:2, :])
    split_mix(anomaly, coef, high_ref, low_ref)
    gain_ref[1] = mixed(high_ref, low_ref, taper_ref[1]).reshape(MEMBERS, MEMBERS, PART)
    middle_gain = gain_ref[0, 0]
    for l in range(1, MEMBERS):
        middle_gain = middle_gain + gain_ref[0, l]
    middle_gain = middle_gain * (1.0 / MEMBERS)

    def compose(l, carry):
        later = gain_ref[1, l]
        total = gain_ref[0, l] + later
        for k in range(MEMBERS):
            total = total + (gain_ref[0, k] - middle_gain) * later[k:k + 1]
        total_ref[l] = total
        return carry

    lax.fori_loop(0, MEMBERS, compose, 0)

    for step in range(STEPS):
        for m in range(2):
            for side in range(2):
                halo(step, m, side).wait_send()
    own.wait()
    for index in range(4):
        near(index).wait_send()
    for offset in order:
        everyone(offset).wait_send()
    for m in range(2):
        for offset in order:
            part(m, offset).wait()

    for k in range(MEMBERS):
        first = (k % 2) * DIRS
        s_ref[k] = state_ref[k // 2, first:first + DIRS, :]
    centre = s_ref[0]
    for k in range(1, MEMBERS):
        centre = centre + s_ref[k]
    centre = centre * (1.0 / MEMBERS)
    for k in range(MEMBERS):
        s_ref[k] = s_ref[k] - centre
    mean_state = e_ref.at[0, 0, 0, pl.ds(0, DIRS), pl.ds(0, PART)]
    mean_state[...] = centre

    for l in range(MEMBERS):
        for tile in range(PART // 128):
            lanes = slice(tile * 128, (tile + 1) * 128)
            total = s_ref[l, :, lanes] + e_ref[0, 0, 0, 0:DIRS, lanes]
            gain = total_ref[l, :, lanes]
            for k in range(MEMBERS):
                total = total + s_ref[k, :, lanes] * gain[k:k + 1]
            count = min(128, OWN - tile * 128)
            out_ref[:, l, tile * 128:tile * 128 + count] = total[:, :count]


def fused(x, speed, turn, trig, cells, values, variances, spaces, peers):
    vmem = pl.BlockSpec(memory_space=pltpu.VMEM)
    dma = pltpu.SemaphoreType.DMA
    return pl.pallas_call(
        functools.partial(wave_kernel, spaces, peers),
        out_shape=jax.ShapeDtypeStruct((DIRS, MEMBERS, OWN), F32),
        in_specs=[vmem] * 7,
        out_specs=vmem,
        scratch_shapes=[
            pltpu.VMEM((STEPS, 2, ROWS, TALL, WIDE), F32),
            pltpu.VMEM((STEPS, 2, HALF, WIDE), F32),
            pltpu.VMEM((STEPS, 2, HALF, WIDE), F32),
            pltpu.VMEM((ROWS, DIRS, WIDE), F32),
            pltpu.VMEM((ROWS, DIRS, WIDE), F32),
            pltpu.VMEM((ROWS, DIRS, WIDE), F32),
            pltpu.VMEM((2 * ROWS, 2 * DIRS, PART), F32),
            pltpu.VMEM((2 * ROWS, WIDE), F32),
            pltpu.VMEM((8, CHUNK), F32),
            pltpu.VMEM((4, 8, CHUNK), F32),
            pltpu.VMEM((8, CHUNK), F32),
            pltpu.VMEM((peers, 2 * DIRS, PART), F32),
            pltpu.VMEM((peers, 8, CHUNK), F32),
            pltpu.VMEM((8, NOBS), F32),
            pltpu.VMEM((NOBS, 8), F32),
            pltpu.VMEM((NOBS, NOBS), BF16),
            pltpu.VMEM((BATCHES, PART, NOBS), BF16),
            pltpu.VMEM((BATCHES * NOBS // CHUNK, WIDE, CHUNK), BF16),
            pltpu.VMEM((MEMBERS, DIRS, PART), F32),
            pltpu.VMEM((MEMBERS, BATCHES * NOBS), F32),
            pltpu.VMEM((MEMBERS, NOBS), F32),
            pltpu.VMEM((MEMBERS * MEMBERS, NOBS), BF16),
            pltpu.VMEM((MEMBERS * MEMBERS, NOBS), BF16),
            pltpu.VMEM((BATCHES, MEMBERS, MEMBERS, PART), F32),
            pltpu.VMEM((MEMBERS, MEMBERS, PART), F32),
            dma((STEPS, 2, 2)), dma((STEPS, 2, 2)),
            dma((2, 8)), dma((2, 8)),
            dma((4,)), dma((4,)),
            dma((8,)), dma((8,)),
            dma(()),
        ],
        compiler_params=pltpu.CompilerParams(collective_id=0, has_side_effects=True),
        name="fused",
    )(x, speed, turn, trig, cells, values, variances)


def per_device(spectra, group_speed, turning_rate, obs_cell, obs_value, obs_variance):
    spaces, peers = lax.axis_size("space"), lax.axis_size("member")
    angles = (2.0 * math.pi * np.arange(DIRS, dtype=np.float32) / DIRS).astype(np.float32)
    trig = np.stack([np.cos(angles), np.sin(angles)]).astype(np.float32)
    trig = np.ascontiguousarray(np.broadcast_to(trig[:, :, None], (2, DIRS, 128)))
    analysis = fused(spectra, group_speed, turning_rate, jnp.asarray(trig), obs_cell, obs_value,
                     obs_variance, spaces, peers)
    return jnp.transpose(analysis, (1, 0, 2))


def solution(mesh):
    placed = (P("member", None, "space", None), P("space", None), P("space", None), P(), P(), P())
    return jax.shard_map(
        per_device,
        mesh=mesh,
        in_specs=placed,
        out_specs=P(None, None, ("space", "member")),
        check_vma=False,
    )
```

```python
import functools
import math

import jax
import jax.numpy as jnp
import numpy as np
from jax import lax
from jax.experimental import pallas as pl
from jax.experimental.pallas import tpu as pltpu
from jax.sharding import PartitionSpec as P

LON = 720
STEPS = 4
BATCHES = 2
LOC = 4
DIRS = 36
NOBS = 1024
MEMBERS = 16
ROWS = 4
OWN = 360
WIDE = 768
TALL = 48
BASE = 8
PART = 384
HALF = 24
CHUNK = 512
F32 = jnp.float32
BF16 = jnp.bfloat16


def step_row(centre, behind, ahead, upwind_y, cx, cy, cr, pick_x):
    west = pltpu.roll(centre, 1, axis=1)
    east = pltpu.roll(centre, WIDE - 1, axis=1)
    result = centre - cx * (centre - jnp.where(pick_x, west, east))
    result = result - cy * (centre - upwind_y)
    return result - jnp.abs(cr) * (centre - jnp.where(cr > 0.0, behind, ahead))


def widen(array):
    return jnp.concatenate([array, array[:, :24], array[:, LON - 24:]], axis=1)


def panel(prior, values, variance):
    centre = jnp.sum(prior, axis=0, keepdims=True) * (1.0 / MEMBERS)
    anomaly = prior - centre
    spread = jnp.sum(anomaly * anomaly, axis=0, keepdims=True) * (1.0 / (MEMBERS - 1))
    total = spread + variance
    shrink = 1.0 / (1.0 + jnp.sqrt(variance / total))
    coef = ((values - centre) - shrink * anomaly) / (total * (MEMBERS - 1))
    return anomaly, coef


def split_mix(anomaly, coef, high_ref, low_ref):
    for l in range(MEMBERS):
        mix = anomaly * coef[l:l + 1]
        high = mix.astype(BF16)
        high_ref[l * MEMBERS:(l + 1) * MEMBERS, :] = high
        low_ref[l * MEMBERS:(l + 1) * MEMBERS, :] = (mix - high.astype(F32)).astype(BF16)


def taper(row, lon, rows, lons):
    lat_gap = row - rows
    lon_gap = jnp.abs(lon - lons)
    lon_gap = jnp.minimum(lon_gap, LON - lon_gap)
    near = jnp.maximum(1.0 - (lat_gap * lat_gap + lon_gap * lon_gap) * (1.0 / (LOC * LOC)), 0.0)
    return (near * near).astype(BF16)


def mixed(high_ref, low_ref, weights):
    dims = (((1,), (1,)), ((), ()))
    return lax.dot_general(
        high_ref[...], weights, dims, preferred_element_type=F32
    ) + lax.dot_general(low_ref[...], weights, dims, preferred_element_type=F32)


def wave_kernel(
    spaces, peers,
    x_ref, speed_ref, turn_ref, trig_ref, cell_ref, value_ref, variance_ref,
    out_ref,
    e_ref, south_ref, north_ref, cx_ref, cy_ref, cr_ref, send_ref, mean_ref,
    mine_ref, near_ref, sum_ref, state_ref, block_ref, place_ref, column_ref,
    cross_ref, taper_ref, onehot_ref, s_ref, prior_ref, next_ref,
    high_ref, low_ref, gain_ref, total_ref,
    halo_send, halo_recv, part_send, part_recv, near_send, near_recv,
    all_send, all_recv, own_sem,
):
    space = lax.axis_index("space")
    member = lax.axis_index("member")
    shifts = (1, spaces - 1, 2, spaces - 2)

    barrier = pltpu.get_barrier_semaphore()
    for shift in shifts:
        pl.semaphore_signal(
            barrier, inc=1, device_id=(lax.rem(space + shift, spaces), member),
            device_id_type=pl.DeviceIdType.MESH)
    for offset in range(1, peers):
        pl.semaphore_signal(
            barrier, inc=1, device_id=(space, lax.rem(member + offset, peers)),
            device_id_type=pl.DeviceIdType.MESH)

    def keep(step, m, r, new):
        e_ref[step, m, r, BASE:BASE + DIRS, :] = new
        e_ref[step, m, r, BASE - 1:BASE, :] = new[DIRS - 1:DIRS]
        e_ref[step, m, r, BASE + DIRS:BASE + DIRS + 1, :] = new[0:1]

    for r in (0, ROWS - 1, 1, 2):
        for m in range(2):
            keep(0, m, r, widen(x_ref[m, :, r, :]))
    pl.semaphore_wait(barrier, len(shifts) + peers - 1)

    def halo(step, m, side):
        if side == 0:
            source = e_ref.at[step, m, ROWS - 1, pl.ds(BASE, HALF)]
            target, to = south_ref.at[step, m], lax.rem(space + 1, spaces)
        else:
            source = e_ref.at[step, m, 0, pl.ds(BASE + 16, HALF)]
            target, to = north_ref.at[step, m], lax.rem(space + spaces - 1, spaces)
        return pltpu.make_async_remote_copy(
            src_ref=source, dst_ref=target,
            send_sem=halo_send.at[step, m, side], recv_sem=halo_recv.at[step, m, side],
            device_id=(to, member), device_id_type=pl.DeviceIdType.MESH)

    for m in range(2):
        for side in range(2):
            halo(0, m, side).start()

    cosines = jnp.concatenate([trig_ref[0]] * (WIDE // 128), axis=1)
    sines = jnp.concatenate([trig_ref[1]] * (WIDE // 128), axis=1)
    speeds = widen(speed_ref[...])
    turns = widen(turn_ref[...])
    for r in range(ROWS):
        cx_ref[r] = speeds[r:r + 1, :] * jnp.abs(cosines)
        cy_ref[r] = speeds[r:r + 1, :] * jnp.abs(sines)
        cr_ref[r] = turns[r:r + 1, :] * cosines
    pick_x = cosines > 0.0
    pick_y = sines > 0.0
    has_south = (space > 0).astype(F32)
    has_north = (space < spaces - 1).astype(F32)

    cells = cell_ref[...].astype(F32)
    rows = jnp.floor((cells + 0.5) * (1.0 / LON))
    lons = cells - rows * float(LON)
    place_ref[...] = jnp.concatenate([rows, lons, rows, lons], axis=0)
    column_ref[...] = jnp.transpose(place_ref[...])

    device = space * peers + member
    own_row = (device // 2).astype(F32)
    own_lon = ((device % 2) * OWN).astype(F32)

    def own_taper(batch):
        cell_lon = lax.broadcasted_iota(jnp.int32, (PART, 128), 0).astype(F32) + own_lon
        cell_lon = jnp.concatenate([cell_lon] * (NOBS // 128), axis=1)
        taper_ref[batch] = taper(own_row, cell_lon, place_ref[batch:batch + 1, :],
                                 place_ref[2 + batch:3 + batch, :])

    width = 256

    def cross_taper(at):
        cross_ref[at:at + width, :] = taper(
            column_ref[at:at + width, 1:2], column_ref[at:at + width, 3:4],
            place_ref[0:1, :], place_ref[2:3, :])

    def select(chunk):
        batch, part_of = divmod(chunk, NOBS // CHUNK)
        lanes = slice(part_of * CHUNK, (part_of + 1) * CHUNK)
        where_lon = lax.broadcasted_iota(jnp.int32, (WIDE, CHUNK), 0).astype(F32)
        onehot_ref[chunk] = jnp.where(
            where_lon == place_ref[2 + batch:3 + batch, lanes], 1.0, 0.0).astype(BF16)

    filler = {
        (0, 0): [lambda: own_taper(0)],
        (0, 1): [lambda: own_taper(1)],
        (1, 0): [lambda: cross_taper(0)],
        (1, 1): [lambda: cross_taper(width)],
        (2, 0): [lambda: cross_taper(2 * width)],
        (2, 1): [lambda: cross_taper(3 * width)],
        (3, 0): [lambda: select(0), lambda: select(1)],
        (3, 1): [lambda: select(2), lambda: select(3)],
    }

    def advance(step, m, r):
        centre = e_ref[step, m, r, BASE:BASE + DIRS, :]
        behind = e_ref[step, m, r, BASE - 1:BASE - 1 + DIRS, :]
        ahead = e_ref[step, m, r, BASE + 1:BASE + 1 + DIRS, :]
        if r > 0:
            south = e_ref[step, m, r - 1, BASE:BASE + DIRS, :]
        if r < ROWS - 1:
            north = e_ref[step, m, r + 1, BASE:BASE + DIRS, :]
        if r == 0:
            south = jnp.concatenate([south_ref[step, m] * has_south, north[HALF:]], axis=0)
        if r == ROWS - 1:
            north = jnp.concatenate(
                [south[:16], (north_ref[step, m] * has_north)[:DIRS - 16]], axis=0)
        new = step_row(centre, behind, ahead, jnp.where(pick_y, south, north),
                       cx_ref[r], cy_ref[r], cr_ref[r], pick_x)
        if step < STEPS - 1:
            keep(step + 1, m, r, new)
        else:
            mean_ref[m * ROWS + r:m * ROWS + r + 1, :] = (
                jnp.sum(new, axis=0, keepdims=True) * (1.0 / DIRS))
            send_ref[2 * r, m * DIRS:(m + 1) * DIRS, :] = new[:, :PART]
            send_ref[2 * r + 1, m * DIRS:(m + 1) * DIRS, :] = pltpu.roll(
                new, WIDE - OWN, axis=1)[:, :PART]

    cuts = ((0, 32), (32, 40))

    def part(m, offset):
        to = lax.rem(member + offset, peers)
        first, count = cuts[m]
        return pltpu.make_async_remote_copy(
            src_ref=send_ref.at[to, pl.ds(first, count)],
            dst_ref=state_ref.at[member, pl.ds(first, count)],
            send_sem=part_send.at[m, offset], recv_sem=part_recv.at[m, offset],
            device_id=(space, to), device_id_type=pl.DeviceIdType.MESH)

    order = (4, 3, 5, 2, 6, 1, 7)
    for step in range(STEPS):
        for m in range(2):
            for r in range(1, ROWS - 1):
                advance(step, m, r)
            for work in filler[(step, m)]:
                work()
            halo(step, m, 0).wait_recv()
            advance(step, m, 0)
            if step < STEPS - 1:
                halo(step + 1, m, 1).start()
            halo(step, m, 1).wait_recv()
            advance(step, m, ROWS - 1)
            if step < STEPS - 1:
                halo(step + 1, m, 0).start()
            elif m == 0:
                for offset in order:
                    part(0, offset).start()

    mean = mean_ref[...]
    high = mean.astype(BF16)
    rest = mean - high.astype(F32)
    middle = rest.astype(BF16)
    low = rest - middle.astype(F32)
    parts = jnp.concatenate([high.astype(F32), middle.astype(F32), low], axis=0).astype(BF16)
    slab = (space * ROWS).astype(F32)
    for chunk in range(BATCHES * NOBS // CHUNK):
        batch, part_of = divmod(chunk, NOBS // CHUNK)
        lanes = slice(part_of * CHUNK, (part_of + 1) * CHUNK)
        onehot = onehot_ref[chunk]
        found = jnp.dot(parts, onehot, preferred_element_type=F32)
        found = found[:8] + found[8:16] + found[16:]
        row = place_ref[batch:batch + 1, lanes] - slab
        for m in range(2):
            value = jnp.zeros((1, CHUNK), F32)
            for r in range(ROWS):
                value = value + jnp.where(row == float(r), found[m * ROWS + r:m * ROWS + r + 1], 0.0)
            mine_ref[m * 4 + chunk:m * 4 + chunk + 1, :] = value

    def near(index):
        return pltpu.make_async_remote_copy(
            src_ref=mine_ref, dst_ref=near_ref.at[index],
            send_sem=near_send.at[index], recv_sem=near_recv.at[index],
            device_id=(lax.rem(space + shifts[index], spaces), member),
            device_id_type=pl.DeviceIdType.MESH)

    for index in range(4):
        near(index).start()
    own = pltpu.make_async_copy(send_ref.at[member], state_ref.at[member], own_sem)
    own.start()
    for index in range(4):
        near(index).wait_recv()
    sum_ref[...] = mine_ref[...] + near_ref[0] + near_ref[1] + near_ref[2] + near_ref[3]
    block_ref[member] = sum_ref[...]

    def everyone(offset):
        return pltpu.make_async_remote_copy(
            src_ref=sum_ref, dst_ref=block_ref.at[member],
            send_sem=all_send.at[offset], recv_sem=all_recv.at[offset],
            device_id=(space, lax.rem(member + offset, peers)),
            device_id_type=pl.DeviceIdType.MESH)

    for offset in order:
        everyone(offset).start()
    for offset in order:
        part(1, offset).start()
    for offset in order:
        everyone(offset).wait_recv()

    for k in range(MEMBERS):
        for chunk in range(4):
            at = (k % 2) * 4 + chunk
            prior_ref[k:k + 1, chunk * CHUNK:(chunk + 1) * CHUNK] = block_ref[k // 2, at:at + 1, :]
    anomaly, coef = panel(prior_ref[:, :NOBS], value_ref[0:1, :], variance_ref[0:1, :])
    split_mix(anomaly, coef, high_ref, low_ref)
    for at in range(0, NOBS, width):
        gain = mixed(high_ref, low_ref, cross_ref[at:at + width, :])
        prior = prior_ref[:, NOBS + at:NOBS + at + width]
        deviation = prior - jnp.sum(prior, axis=0, keepdims=True) * (1.0 / MEMBERS)
        for l in range(MEMBERS):
            next_ref[l:l + 1, at:at + width] = prior[l:l + 1] + jnp.sum(
                deviation * gain[l * MEMBERS:(l + 1) * MEMBERS], axis=0, keepdims=True)
    gain_ref[0] = mixed(high_ref, low_ref, taper_ref[0]).reshape(MEMBERS, MEMBERS, PART)
    anomaly, coef = panel(next_ref[...], value_ref[1:2, :], variance_ref[1:2, :])
    split_mix(anomaly, coef, high_ref, low_ref)
    gain_ref[1] = mixed(high_ref, low_ref, taper_ref[1]).reshape(MEMBERS, MEMBERS, PART)
    middle_gain = gain_ref[0, 0]
    for l in range(1, MEMBERS):
        middle_gain = middle_gain + gain_ref[0, l]
    middle_gain = middle_gain * (1.0 / MEMBERS)

    def compose(l, carry):
        later = gain_ref[1, l]
        total = gain_ref[0, l] + later
        for k in range(MEMBERS):
            total = total + (gain_ref[0, k] - middle_gain) * later[k:k + 1]
        total_ref[l] = total
        return carry

    lax.fori_loop(0, MEMBERS, compose, 0)

    for step in range(STEPS):
        for m in range(2):
            for side in range(2):
                halo(step, m, side).wait_send()
    own.wait()
    for index in range(4):
        near(index).wait_send()
    for offset in order:
        everyone(offset).wait_send()
    for m in range(2):
        for offset in order:
            part(m, offset).wait()

    for k in range(MEMBERS):
        first = (k % 2) * DIRS
        s_ref[k] = state_ref[k // 2, first:first + DIRS, :]
    centre = s_ref[0]
    for k in range(1, MEMBERS):
        centre = centre + s_ref[k]
    centre = centre * (1.0 / MEMBERS)
    for k in range(MEMBERS):
        s_ref[k] = s_ref[k] - centre
    mean_state = e_ref.at[0, 0, 0, pl.ds(0, DIRS), pl.ds(0, PART)]
    mean_state[...] = centre

    for l in range(MEMBERS):
        for tile in range(PART // 128):
            lanes = slice(tile * 128, (tile + 1) * 128)
            total = s_ref[l, :, lanes] + e_ref[0, 0, 0, 0:DIRS, lanes]
            gain = total_ref[l, :, lanes]
            for k in range(MEMBERS):
                total = total + s_ref[k, :, lanes] * gain[k:k + 1]
            count = min(128, OWN - tile * 128)
            out_ref[:, l, tile * 128:tile * 128 + count] = total[:, :count]


def fused(x, speed, turn, trig, cells, values, variances, spaces, peers):
    vmem = pl.BlockSpec(memory_space=pltpu.VMEM)
    dma = pltpu.SemaphoreType.DMA
    return pl.pallas_call(
        functools.partial(wave_kernel, spaces, peers),
        out_shape=jax.ShapeDtypeStruct((DIRS, MEMBERS, OWN), F32),
        in_specs=[vmem] * 7,
        out_specs=vmem,
        scratch_shapes=[
            pltpu.VMEM((STEPS, 2, ROWS, TALL, WIDE), F32),
            pltpu.VMEM((STEPS, 2, HALF, WIDE), F32),
            pltpu.VMEM((STEPS, 2, HALF, WIDE), F32),
            pltpu.VMEM((ROWS, DIRS, WIDE), F32),
            pltpu.VMEM((ROWS, DIRS, WIDE), F32),
            pltpu.VMEM((ROWS, DIRS, WIDE), F32),
            pltpu.VMEM((2 * ROWS, 2 * DIRS, PART), F32),
            pltpu.VMEM((2 * ROWS, WIDE), F32),
            pltpu.VMEM((8, CHUNK), F32),
            pltpu.VMEM((4, 8, CHUNK), F32),
            pltpu.VMEM((8, CHUNK), F32),
            pltpu.VMEM((peers, 2 * DIRS, PART), F32),
            pltpu.VMEM((peers, 8, CHUNK), F32),
            pltpu.VMEM((8, NOBS), F32),
            pltpu.VMEM((NOBS, 8), F32),
            pltpu.VMEM((NOBS, NOBS), BF16),
            pltpu.VMEM((BATCHES, PART, NOBS), BF16),
            pltpu.VMEM((BATCHES * NOBS // CHUNK, WIDE, CHUNK), BF16),
            pltpu.VMEM((MEMBERS, DIRS, PART), F32),
            pltpu.VMEM((MEMBERS, BATCHES * NOBS), F32),
            pltpu.VMEM((MEMBERS, NOBS), F32),
            pltpu.VMEM((MEMBERS * MEMBERS, NOBS), BF16),
            pltpu.VMEM((MEMBERS * MEMBERS, NOBS), BF16),
            pltpu.VMEM((BATCHES, MEMBERS, MEMBERS, PART), F32),
            pltpu.VMEM((MEMBERS, MEMBERS, PART), F32),
            dma((STEPS, 2, 2)), dma((STEPS, 2, 2)),
            dma((2, 8)), dma((2, 8)),
            dma((4,)), dma((4,)),
            dma((8,)), dma((8,)),
            dma(()),
        ],
        compiler_params=pltpu.CompilerParams(collective_id=0, has_side_effects=True),
        name="fused",
    )(x, speed, turn, trig, cells, values, variances)


def per_device(spectra, group_speed, turning_rate, obs_cell, obs_value, obs_variance):
    spaces, peers = lax.axis_size("space"), lax.axis_size("member")
    angles = (2.0 * math.pi * np.arange(DIRS, dtype=np.float32) / DIRS).astype(np.float32)
    trig = np.stack([np.cos(angles), np.sin(angles)]).astype(np.float32)
    trig = np.ascontiguousarray(np.broadcast_to(trig[:, :, None], (2, DIRS, 128)))
    analysis = fused(spectra, group_speed, turning_rate, jnp.asarray(trig), obs_cell, obs_value,
                     obs_variance, spaces, peers)
    return jnp.transpose(analysis, (1, 0, 2))


def solution(mesh):
    placed = (P("member", None, "space", None), P("space", None), P("space", None), P(), P(), P())
    return jax.shard_map(
        per_device,
        mesh=mesh,
        in_specs=placed,
        out_specs=P(None, None, ("space", "member")),
        check_vma=False,
    )
```
